128 devices in a mesh: dp: 4 (over z), seq: 32 (over x, y, core).
Axes of the slice: x: 4, y: 4, z: 4, core: 2. Of those that a mesh axis runs over, the one named last changes fastest.
Arguments:
- queries: bfloat16 [4, 4096, 12288], P('dp', 'seq'), may hold values from -8 to 8
- keys_in: bfloat16 [4, 4096, 768], P('dp', 'seq'), may hold values from -8 to 8
- values_in: bfloat16 [4, 4096, 512], P('dp', 'seq'), may hold values from -6 to 6
- gate_cmp: float32 [4, 4096, 64], P('dp', 'seq'), may hold values from 0.05 to 0.95
- gate_win: float32 [4, 4096, 64], P('dp', 'seq'), may hold values from 0.05 to 0.95
- cotangent: bfloat16 [4, 4096, 8192], P('dp', 'seq'), may hold values from -6 to 6
- compress_key: bfloat16 [6144, 192], replicated, may hold values from -1 to 1
- compress_value: bfloat16 [4096, 128], replicated, may hold values from -0.09375 to 0.09375
Outputs:
- attended: bfloat16 [4, 4096, 8192], P('dp', 'seq')
- grad_query: bfloat16 [4, 4096, 12288], P('dp', 'seq')
- grad_key: bfloat16 [4, 4096, 768], P('dp', 'seq')
- grad_value: bfloat16 [4, 4096, 512], P('dp', 'seq')
- grad_gate_cmp: float32 [4, 4096, 64], P('dp', 'seq')
- grad_gate_win: float32 [4, 4096, 64], P('dp', 'seq')
- grad_compress_key: float32 [6144, 192], P('seq')
- grad_compress_value: float32 [4096, 128], P('seq')
The draws below stay inside these ranges and needn't reach their ends.
All inputs are finite; a program needn't handle non-finite values.
Results may differ from the reference program's by a relative error of at most 0.023.
Values may be sent and summed in bfloat16 or wider, within the bound.
No kernel may reach another device: no remote copies, remote signals or barrier semaphores. Data moves between devices by JAX's collectives and lax.ppermute only.
A program may use at most 192 MiB of HBM per device.

```python
import math
import jax
import jax.numpy as jnp
from jax import lax

H = 64
G = 4
DH = 192
DV = 128
BLK = 32
STRIDE = 16
WIN = 512
TOK_DEV = 128
SEQ = 4096
BATCH = 4


def draw_queries(key, part):
    base_draw = jax.random.truncated_normal(jax.random.fold_in(key, 21), -6.0, 6.0, (BATCH, SEQ, H * DH), jnp.float32)
    return base_draw.astype(jnp.bfloat16)


def draw_keys_in(key, part):
    base_draw = jax.random.truncated_normal(jax.random.fold_in(key, 22), -6.0, 6.0, (BATCH, SEQ, G * DH), jnp.float32)
    return base_draw.astype(jnp.bfloat16)


def draw_compress_key(key, part):
    base_draw = jax.random.truncated_normal(jax.random.fold_in(key, 23), -6.0, 6.0, (BLK * DH, DH), jnp.float32) / math.sqrt(BLK * DH)
    return base_draw.astype(jnp.bfloat16)


def levels(rng, shape, cuts, low, largest):
    def one(axis_at, shards_of):
        draws = jax.random.uniform(jax.random.fold_in(jax.random.fold_in(rng, 6), axis_at), (shards_of,), jnp.float32, low / len(cuts), largest / len(cuts))
        return jnp.repeat(jnp.exp(draws), shape[axis_at] // shards_of).reshape((-1,) + (1,) * (len(shape) - axis_at - 1))

    gain = one(*cuts[0])
    for cut in cuts[1:]:
        gain = gain * one(*cut)
    return gain


def scatter_about(stream_key, dims, scale, limit, split=(), kind=jnp.bfloat16):
    factor_of = levels(stream_key, dims, split, -0.22, 0.18) if split else 1.0
    array = jax.random.normal(stream_key, dims, jnp.float32) * scale * factor_of
    return jnp.minimum(jnp.maximum(array, -limit), limit).astype(kind)


def setup_inputs(seed: int = 0) -> dict:
    keys = jax.random.split(jax.random.key(seed), 9)
    return {
        "queries": draw_queries(jax.random.fold_in(keys[8], 71), 0),
        "keys_in": draw_keys_in(jax.random.fold_in(keys[8], 71), 0),
        "values_in": scatter_about(keys[2], (BATCH, SEQ, G * DV), 1.0, 6.0, ((0, 4), (1, 32))),
        "gate_cmp": jnp.clip(0.05 + 0.9 * jax.random.uniform(keys[3], (BATCH, SEQ, H), jnp.float32) ** levels(keys[3], (BATCH, SEQ, H), ((0, 4), (1, 32)), -0.2, 0.2), 0.05, 0.95),
        "gate_win": jnp.clip(0.05 + 0.9 * jax.random.uniform(keys[4], (BATCH, SEQ, H), jnp.float32) ** levels(keys[4], (BATCH, SEQ, H), ((0, 4), (1, 32)), -0.2, 0.2), 0.05, 0.95),
        "cotangent": scatter_about(keys[5], (BATCH, SEQ, H * DV), 1.0, 6.0, ((0, 4), (1, 32))),
        "compress_key": draw_compress_key(jax.random.fold_in(keys[8], 71), 0),
        "compress_value": scatter_about(keys[7], (BLK * DV, DV), (BLK * DV) ** -0.5, 0.09375),
    }


def attend(query_b, keys_b, values_b, valid, gate_vals, cotangent_b):
    scaling = 1.0 / math.sqrt(query_b.shape[-1])
    query_f = query_b.astype(jnp.float32)
    keys_f = keys_b.astype(jnp.float32)
    values_f = values_b.astype(jnp.float32)
    scores = jnp.einsum('tgcd,kgd->tgck', query_f, keys_f) * scaling
    scores = jnp.where(valid[:, None, None, :], scores, -1e+30)
    row_max = lax.optimization_barrier(jnp.max(scores, axis=-1, keepdims=True))
    exponent = jnp.exp(scores - row_max)
    softmax_w = exponent / lax.optimization_barrier(jnp.sum(exponent, axis=-1, keepdims=True))
    softmax_b = softmax_w.astype(jnp.bfloat16).astype(jnp.float32)
    branch_out = jnp.einsum('tgck,kgd->tgcd', softmax_b, values_f)
    cotangent_f = cotangent_b.astype(jnp.float32)
    grad_gate = lax.optimization_barrier(jnp.sum(cotangent_f * branch_out, axis=-1))
    grad_out = (gate_vals[..., None] * cotangent_f).astype(jnp.bfloat16).astype(jnp.float32)
    grad_v = jnp.einsum('tgck,tgcd->kgd', softmax_b, grad_out)
    grad_prob = jnp.einsum('tgcd,kgd->tgck', grad_out, values_f)
    row_delta = lax.optimization_barrier(jnp.sum(grad_out * branch_out, axis=-1, keepdims=True))
    grad_score = (softmax_w * (grad_prob - row_delta) * scaling).astype(jnp.bfloat16).astype(jnp.float32)
    grad_q = jnp.einsum('tgck,kgd->tgcd', grad_score, keys_f)
    grad_k = jnp.einsum('tgck,tgcd->kgd', grad_score, query_f)
    return (branch_out, grad_gate, grad_q, grad_k, grad_v)

def compress(keys_b, weight):
    width = keys_b.shape[1]
    head_dim = weight.shape[1]
    groups = width // head_dim
    padded = jnp.concatenate([jnp.zeros((BLK, width), jnp.bfloat16), keys_b[:SEQ - STRIDE]], axis=0)
    halves = padded.reshape(-1, STRIDE, groups, head_dim)
    blocks = jnp.concatenate([halves[:-1], halves[1:]], axis=1)
    weight_cube = weight.reshape(BLK, head_dim, head_dim).astype(jnp.float32)
    compressed = jnp.einsum('bpgd,pde->bge', blocks.astype(jnp.float32), weight_cube).astype(jnp.bfloat16)
    return (blocks, compressed)

def compress_back(blocks, weight, grad_blocks):
    groups = blocks.shape[2]
    head_dim = weight.shape[1]
    weight_cube = weight.reshape(BLK, head_dim, head_dim).astype(jnp.float32)
    grad_round = grad_blocks.astype(jnp.bfloat16).astype(jnp.float32)
    grad_slabs = jnp.einsum('bge,pde->bpgd', grad_round, weight_cube)
    grad_weight = jnp.einsum('bpgd,bge->pde', blocks.astype(jnp.float32), grad_round).reshape(BLK * head_dim, head_dim)
    zero_half = jnp.zeros((1, STRIDE, groups, head_dim), jnp.float32)
    grad_halves = jnp.concatenate([grad_slabs[:, :STRIDE], zero_half], axis=0) + jnp.concatenate([zero_half, grad_slabs[:, STRIDE:]], axis=0)
    grad_padded = grad_halves.reshape(-1, groups * head_dim)
    grad_tokens = jnp.concatenate([grad_padded[BLK:], jnp.zeros((STRIDE, groups * head_dim), jnp.float32)], axis=0)
    return (grad_tokens, grad_weight)

def one_sequence(queries, keys_in, values_in, gate_cmp, gate_win, cotangent, compress_key, compress_value):
    kv_width = keys_in.shape[1]
    value_width = values_in.shape[1]
    groups = kv_width // DH
    per_group = H // groups
    reach_shards = (WIN + TOK_DEV - 1) // TOK_DEV
    lead_count = reach_shards * TOK_DEV
    key_count = lead_count + TOK_DEV
    key_blocks, cmp_keys = compress(keys_in, compress_key)
    value_blocks, cmp_values = compress(values_in, compress_value)
    block_count = cmp_keys.shape[0]
    keys_wide = jnp.concatenate([jnp.zeros((lead_count, kv_width), jnp.bfloat16), keys_in], axis=0).reshape(-1, groups, DH)
    values_wide = jnp.concatenate([jnp.zeros((lead_count, value_width), jnp.bfloat16), values_in], axis=0).reshape(-1, groups, DV)

    def step_block(totals, block_index):
        grad_kw, grad_vw, grad_ck, grad_cv = totals
        first_row = block_index * TOK_DEV
        query_b = lax.dynamic_slice_in_dim(queries, first_row, TOK_DEV, 0).reshape(TOK_DEV, groups, per_group, DH)
        cotangent_b = lax.dynamic_slice_in_dim(cotangent, first_row, TOK_DEV, 0).reshape(TOK_DEV, groups, per_group, DV)
        gate_c = lax.dynamic_slice_in_dim(gate_cmp, first_row, TOK_DEV, 0).reshape(TOK_DEV, groups, per_group)
        gate_w = lax.dynamic_slice_in_dim(gate_win, first_row, TOK_DEV, 0).reshape(TOK_DEV, groups, per_group)
        window_k = lax.dynamic_slice_in_dim(keys_wide, first_row, key_count, 0)
        window_v = lax.dynamic_slice_in_dim(values_wide, first_row, key_count, 0)
        query_pos = first_row + jnp.arange(TOK_DEV, dtype=jnp.int32)
        key_pos = first_row - lead_count + jnp.arange(key_count, dtype=jnp.int32)
        distance = query_pos[:, None] - key_pos[None, :]
        window_mask = (key_pos[None, :] >= 0) & (distance >= 0) & (distance < WIN)
        causal_mask = STRIDE * jnp.arange(block_count, dtype=jnp.int32)[None, :] <= query_pos[:, None] + 1
        out_cmp, gate_grad_c, grad_q_c, grad_k_c, grad_v_c = attend(query_b, cmp_keys, cmp_values, causal_mask, gate_c, cotangent_b)
        out_win, gate_grad_w, grad_q_w, grad_k_w, grad_v_w = attend(query_b, window_k, window_v, window_mask, gate_w, cotangent_b)
        out_block = (gate_c[..., None] * out_cmp + gate_w[..., None] * out_win).astype(jnp.bfloat16).reshape(TOK_DEV, -1)
        grad_q_block = (grad_q_c + grad_q_w).astype(jnp.bfloat16).reshape(TOK_DEV, -1)
        grad_kw = lax.dynamic_update_slice_in_dim(grad_kw, lax.dynamic_slice_in_dim(grad_kw, first_row, key_count, 0) + grad_k_w.reshape(key_count, kv_width), first_row, 0)
        grad_vw = lax.dynamic_update_slice_in_dim(grad_vw, lax.dynamic_slice_in_dim(grad_vw, first_row, key_count, 0) + grad_v_w.reshape(key_count, value_width), first_row, 0)
        totals = (grad_kw, grad_vw, grad_ck + grad_k_c, grad_cv + grad_v_c)
        return (totals, (out_block, grad_q_block, gate_grad_c.reshape(TOK_DEV, -1), gate_grad_w.reshape(TOK_DEV, -1)))
    start_totals = (jnp.zeros((lead_count + SEQ, kv_width), jnp.float32), jnp.zeros((lead_count + SEQ, value_width), jnp.float32), jnp.zeros((block_count, groups, DH), jnp.float32), jnp.zeros((block_count, groups, DV), jnp.float32))
    totals, stacked = lax.scan(step_block, start_totals, jnp.arange(SEQ // TOK_DEV, dtype=jnp.int32))
    grad_kw, grad_vw, grad_ck, grad_cv = totals
    grad_k_cmp, grad_wk = compress_back(key_blocks, compress_key, grad_ck)
    grad_v_cmp, grad_wv = compress_back(value_blocks, compress_value, grad_cv)
    grad_key = (grad_kw[lead_count:] + grad_k_cmp).astype(jnp.bfloat16)
    grad_value = (grad_vw[lead_count:] + grad_v_cmp).astype(jnp.bfloat16)
    attended = stacked[0].reshape(SEQ, -1)
    grad_query = stacked[1].reshape(SEQ, -1)
    return (attended, grad_query, grad_key, grad_value, stacked[2].reshape(SEQ, -1), stacked[3].reshape(SEQ, -1), grad_wk, grad_wv)

def sum_list(arrays):
    total = arrays[0]
    for other in arrays[1:]:
        total = total + other
    return total

def reference(queries, keys_in, values_in, gate_cmp, gate_win, cotangent, compress_key, compress_value):
    results = []
    for seq_index in range(BATCH):
        results.append(one_sequence(queries[seq_index], keys_in[seq_index], values_in[seq_index], gate_cmp[seq_index], gate_win[seq_index], cotangent[seq_index], compress_key, compress_value))
    stacked = [jnp.stack([item[slot] for item in results]) for slot in range(6)]
    grad_wk = sum_list([item[6] for item in results])
    grad_wv = sum_list([item[7] for item in results])
    return (stacked[0], stacked[1], stacked[2], stacked[3], stacked[4], stacked[5], grad_wk, grad_wv)
```

```python
import functools
import functools
import math
import jax
import jax.numpy as jnp
from jax import lax
from jax.experimental import pallas as pl
from jax.experimental.pallas import tpu as pltpu
from jax.sharding import PartitionSpec as P


BLK = 32
STRIDE = 16
WIN = 512
NEG = -1e30
QB = 32


def stack_rows(ref, row, width, starts):
    parts = [ref[row : row + QB, at : at + width] for at in starts]
    return jnp.concatenate(parts, axis=0)


def nt(a, b):
    return lax.dot_general(a, b, (((1,), (1,)), ((), ())), preferred_element_type=jnp.float32)


def nn(a, b):
    return lax.dot_general(a, b, (((1,), (0,)), ((), ())), preferred_element_type=jnp.float32)


def lay_keys(pair, ke, ko, kt, rows, odd_group, dh):
    def even():
        lane = lax.broadcasted_iota(jnp.int32, (pair.shape[0], 256), 1)
        src = pair[:, :256].astype(jnp.float32)
        low = jnp.where(lane < dh, src, 0.0)
        ke[rows, :] = low.astype(jnp.bfloat16)
        ko[rows, :] = pltpu.roll(low, 256 - dh, 1).astype(jnp.bfloat16)
        kt[:, rows] = low.T[:dh].astype(jnp.bfloat16)

    def odd():
        lane = lax.broadcasted_iota(jnp.int32, (pair.shape[0], 256), 1)
        src = pair[:, 128:].astype(jnp.float32)
        high = jnp.where(lane >= 256 - dh, src, 0.0)
        low = pltpu.roll(high, dh, 1)
        ko[rows, :] = high.astype(jnp.bfloat16)
        ke[rows, :] = low.astype(jnp.bfloat16)
        kt[:, rows] = low.T[:dh].astype(jnp.bfloat16)

    pl.when(jnp.logical_not(odd_group))(even)
    pl.when(odd_group)(odd)


def join_keys_grad(acc_e, acc_o, scale, dh, odd_group, put):
    def even():
        lane = lax.broadcasted_iota(jnp.int32, acc_e.shape, 1)
        total = (acc_e[...] + pltpu.roll(acc_o[...], dh, 1)) * scale
        put(0, jnp.where(lane < dh, total, 0.0), False)

    def odd():
        lane = lax.broadcasted_iota(jnp.int32, acc_e.shape, 1)
        total = (acc_o[...] + pltpu.roll(acc_e[...], 256 - dh, 1)) * scale
        put(128, jnp.where(lane >= 256 - dh, total, 0.0), True)

    pl.when(jnp.logical_not(odd_group))(even)
    pl.when(odd_group)(odd)


def unit(qs, cs, gate, kx, vv, kt, vt, chunks, mask, valid, s_scr, g_scr, p_scr, u_scr, acc_k, acc_v, scale):
    to_log2 = scale * math.log2(math.e)
    first, last = chunks[0][0], chunks[-1][1]
    total = s_scr.shape[0]
    tops = []
    for at, end in chunks:
        s = mask(nt(kx[at:end, :], qs) * to_log2, at, end)
        s_scr[at:end, :] = s
        top = jnp.max(s, axis=0, keepdims=True)
        ok = valid(at)
        tops.append(top if ok is None else jnp.where(ok, top, NEG))
    top = tops[0]
    for other in tops[1:]:
        top = jnp.maximum(top, other)
    norm = jnp.zeros_like(top)
    mean = jnp.zeros_like(top)
    for at, end in chunks:
        ok = valid(at)
        base = top if ok is None else jnp.where(ok, top, -NEG)
        e = jnp.exp2(s_scr[at:end, :] - base)
        gp = nt(vv[at:end, :], cs)
        s_scr[at:end, :] = e
        g_scr[at:end, :] = gp
        norm = norm + jnp.sum(e, axis=0, keepdims=True)
        mean = mean + jnp.sum(e * gp, axis=0, keepdims=True)
    mean = mean / norm
    weight = gate / norm
    for at, end in chunks:
        p = s_scr[at:end, :] * weight
        u = (p * (g_scr[at:end, :] - mean)).astype(jnp.bfloat16)
        pb = p.astype(jnp.bfloat16)
        p_scr[at:end, :] = pb
        u_scr[at:end, :] = u
        acc_v[at:end, :] += nn(pb, cs)
        acc_k[at:end, :] += nn(u, qs)
    for lo, hi in ((0, first), (last, total)):
        if hi > lo:
            p_scr[lo:hi, :] = jnp.zeros((hi - lo, 256), jnp.bfloat16)
            u_scr[lo:hi, :] = jnp.zeros((hi - lo, 256), jnp.bfloat16)
    out = nn(vt[...], p_scr[...])
    dq = nn(kt[...], u_scr[...]) * scale
    return out, dq, mean


def cmp_kernel(first_ref, q_ref, c_ref, gate_ref, ck_ref, cv_ref, o_ref, dq_ref, gg_ref, gk_ref,
               ke, ko, kt, vt, s_e, s_o, g_e, g_o, p_e, p_o, u_e, u_o, acc_e, acc_o, acc_v, acc_w, *, dh, dv):
    group = pl.program_id(0)
    odd_group = group % 2 == 1
    scale = 1.0 / math.sqrt(dh)
    rows = ck_ref.shape[0]
    tokens = q_ref.shape[0]
    lay_keys(ck_ref, ke, ko, kt, slice(0, rows), odd_group, dh)
    vt[...] = cv_ref[...].astype(jnp.float32).T.astype(jnp.bfloat16)
    for acc in (acc_e, acc_o, acc_v, acc_w):
        acc[...] = jnp.zeros_like(acc)
    chunks = [(at, at + 128) for at in range(0, rows, 128)]
    heads = q_ref.shape[1] // dh // 2
    for block in range(tokens // QB):
        row = block * QB
        lane = lax.broadcasted_iota(jnp.int32, (1, 256), 1) & (QB - 1)
        limit = (first_ref[0] + row + 1 + lane) // STRIDE

        def mask(s, at, end):
            index = at + lax.broadcasted_iota(jnp.int32, (end - at, 256), 0)
            return jnp.where(index <= limit, s, NEG)

        for par, (kx, s, g, p, u, acc, accv) in enumerate(((ke, s_e, g_e, p_e, u_e, acc_e, acc_v), (ko, s_o, g_o, p_o, u_o, acc_o, acc_w))):
            qs = stack_rows(q_ref, row, 256, [2 * dh * h + par * 128 for h in range(heads)])
            cs = stack_rows(c_ref, row, dv, [(2 * h + par) * dv for h in range(heads)])
            at = 2 * block + par
            out, dq, mean = unit(qs, cs, gate_ref[0, at : at + 1, :], kx, cv_ref, kt, vt, chunks, mask,
                                 lambda at: None, s, g, p, u, acc, accv, scale)
            gg_ref[0, at : at + 1, :] = mean
            o_ref[0, at] = out.astype(jnp.bfloat16)
            dq_ref[0, block, par * dh : (par + 1) * dh, :] = dq.astype(jnp.bfloat16)
    base = pl.multiple_of((group // 2) * 2 * dh, 128)

    def put(at, value, add):
        if add:
            gk_ref[:, pl.ds(base + at, 128)] = (gk_ref[:, pl.ds(base + at, 128)].astype(jnp.float32) + value[:, :128]).astype(jnp.bfloat16)
            gk_ref[:, pl.ds(base + at + 128, 128)] = value[:, 128:].astype(jnp.bfloat16)
        else:
            gk_ref[:, pl.ds(base + at, 256)] = value.astype(jnp.bfloat16)

    join_keys_grad(acc_e, acc_o, scale, dh, odd_group, put)
    at = pl.multiple_of(4 * dh + group * dv, 128)
    gk_ref[:, pl.ds(at, dv)] = (acc_v[...] + acc_w[...]).astype(jnp.bfloat16)


def win_kernel(start_ref, q_ref, c_ref, gate_ref, k_ref, v_ref, h4, h3, h2, h1, oc_ref, dqc_ref, *refs, dh, dv, pair):
    refs = refs[2:] if pair else refs
    win_body(start_ref, q_ref, c_ref, gate_ref, k_ref, v_ref, (h4, h3, h2, h1), oc_ref, dqc_ref, *refs, dh=dh, dv=dv, pair=pair)


def win_body(start_ref, q_ref, c_ref, gate_ref, k_ref, v_ref, halo_refs, oc_ref, dqc_ref,
             o_ref, dq_ref, gg_ref, gh_ref, gown_ref,
               ke, ko, vv, kt, vt, s_e, s_o, g_e, g_o, p_e, p_o, u_e, u_o, acc_e, acc_o, acc_v, acc_w, *, dh, dv, pair):
    odd_group = pl.program_id(0) == 1
    scale = 1.0 / math.sqrt(dh)
    tokens = q_ref.shape[0]
    lead = WIN
    base = pair * 2 * dh
    vbase = pl.multiple_of(4 * dh + (2 * pair + pl.program_id(0)) * dv, 128)
    for n, h in enumerate(halo_refs):
        rows = slice(n * tokens, (n + 1) * tokens)
        lay_keys(h[:, pl.ds(base, 2 * dh)], ke, ko, kt, rows, odd_group, dh)
        vv[rows, :] = h[:, pl.ds(vbase, dv)]
    lay_keys(k_ref, ke, ko, kt, slice(lead, lead + tokens), odd_group, dh)
    vv[lead:, :] = v_ref[...]
    vt[...] = vv[...].astype(jnp.float32).T.astype(jnp.bfloat16)
    for acc in (acc_e, acc_o, acc_v, acc_w):
        acc[...] = jnp.zeros_like(acc)
    heads = q_ref.shape[1] // dh // 2

    def valid(at):
        return None if at >= lead else at >= start_ref[0]

    for block in range(tokens // QB):
        row = block * QB
        edges = sorted({row, row + QB, 128, 256, 384, 512, lead + row, lead + row + QB} - {0})
        edges = [row] + [x for x in edges if row < x <= lead + row + QB]
        chunks = list(zip(edges[:-1], edges[1:]))
        lane = lax.broadcasted_iota(jnp.int32, (QB, 256), 1) & (QB - 1)
        sub = lax.broadcasted_iota(jnp.int32, (QB, 256), 0)

        def mask(s, at, end):
            if at == row and end == row + QB:
                return jnp.where(sub > lane, s, NEG)
            if at == lead + row:
                return jnp.where(sub <= lane, s, NEG)
            return s

        dqs = []
        for par, (kx, s, g, p, u, acc, accv) in enumerate(((ke, s_e, g_e, p_e, u_e, acc_e, acc_v), (ko, s_o, g_o, p_o, u_o, acc_o, acc_w))):
            qs = stack_rows(q_ref, row, 256, [2 * dh * h + par * 128 for h in range(heads)])
            cs = stack_rows(c_ref, row, dv, [(2 * h + par) * dv for h in range(heads)])
            at = 2 * block + par
            out, dq, mean = unit(qs, cs, gate_ref[0, at : at + 1, :], kx, vv, kt, vt, chunks, mask,
                                 valid, s, g, p, u, acc, accv, scale)
            gg_ref[0, at : at + 1, :] = mean
            out = (out + oc_ref[0, at].astype(jnp.float32)).T
            for h in range(heads):
                o_ref[row : row + QB, (2 * h + par) * dv : (2 * h + par + 1) * dv] = out[h * QB : (h + 1) * QB].astype(jnp.bfloat16)
            dqs.append(dq + dqc_ref[0, block, par * dh : (par + 1) * dh, :].astype(jnp.float32))
        dq = jnp.concatenate(dqs, axis=0).T
        for h in range(heads):
            dq_ref[row : row + QB, 2 * dh * h : 2 * dh * (h + 1)] = dq[h * QB : (h + 1) * QB].astype(jnp.bfloat16)

    def put(at, value, add):
        for ref, lo, hi, kind in ((gh_ref, 0, lead, jnp.bfloat16), (gown_ref, lead, lead + tokens, jnp.float32)):
            part = value[lo:hi]
            if add:
                ref[:, at : at + 128] = (ref[:, at : at + 128].astype(jnp.float32) + part[:, :128]).astype(kind)
                ref[:, at + 128 : at + 256] = part[:, 128:].astype(kind)
            else:
                ref[:, at : at + 256] = part.astype(kind)

    join_keys_grad(acc_e, acc_o, scale, dh, odd_group, put)
    total = acc_v[...] + acc_w[...]
    vat = pl.multiple_of(2 * dh + pl.program_id(0) * dv, 128)
    gh_ref[:, pl.ds(vat, dv)] = total[:lead].astype(jnp.bfloat16)
    gown_ref[:, pl.ds(vat, dv)] = total[lead:]


def scratch(keys, dh, dv, own_values):
    f32, b16 = jnp.float32, jnp.bfloat16
    return [
        pltpu.VMEM((keys, 256), b16), pltpu.VMEM((keys, 256), b16),
        *([pltpu.VMEM((keys, dv), b16)] if own_values else []),
        pltpu.VMEM((dh, keys), b16), pltpu.VMEM((dv, keys), b16),
        *[pltpu.VMEM((keys, 256), f32)] * 4, *[pltpu.VMEM((keys, 256), b16)] * 4,
        pltpu.VMEM((keys, 256), f32), pltpu.VMEM((keys, 256), f32),
        pltpu.VMEM((keys, dv), f32), pltpu.VMEM((keys, dv), f32),
    ]


def attend_cmp(first, q, c, gate, ckv, groups, dh, dv):
    tokens, blocks = q.shape[0], ckv.shape[0]
    skip = groups * dh // dv
    wide, high = q.shape[1] // groups, c.shape[1] // groups
    steps = tokens // QB
    f32, b16 = jnp.float32, jnp.bfloat16
    return pl.pallas_call(
        functools.partial(cmp_kernel, dh=dh, dv=dv),
        grid=(groups,),
        in_specs=[
            pl.BlockSpec(memory_space=pltpu.SMEM),
            pl.BlockSpec((tokens, wide), lambda g: (0, g)),
            pl.BlockSpec((tokens, high), lambda g: (0, g)),
            pl.BlockSpec((1, 2 * steps, 256), lambda g: (g, 0, 0)),
            pl.BlockSpec((blocks, 2 * dh), lambda g: (0, g // 2)),
            pl.BlockSpec((blocks, dv), lambda g: (0, skip + g)),
        ],
        out_specs=[
            pl.BlockSpec((1, 2 * steps, dv, 256), lambda g: (g, 0, 0, 0)),
            pl.BlockSpec((1, steps, 2 * dh, 256), lambda g: (g, 0, 0, 0)),
            pl.BlockSpec((1, 2 * steps, 256), lambda g: (g, 0, 0)),
            pl.BlockSpec((blocks, groups * (dh + dv)), lambda g: (0, 0)),
        ],
        out_shape=[
            jax.ShapeDtypeStruct((groups, 2 * steps, dv, 256), b16),
            jax.ShapeDtypeStruct((groups, steps, 2 * dh, 256), b16),
            jax.ShapeDtypeStruct((groups, 2 * steps, 256), f32),
            jax.ShapeDtypeStruct((blocks, groups * (dh + dv)), b16),
        ],
        scratch_shapes=scratch(blocks, dh, dv, False),
        compiler_params=pltpu.CompilerParams(dimension_semantics=("arbitrary",), vmem_limit_bytes=56 * 2**20),
        cost_estimate=pl.CostEstimate(flops=blocks * tokens * 64 * 1920, transcendentals=blocks * tokens * 64, bytes_accessed=30_000_000),
        name="attend_cmp",
    )(first, q, c, gate, ckv, ckv)


def attend_win(start, q, c, gate, k, v, halos, oc, dqc, groups, dh, dv, pair, before):
    tokens = q.shape[0]
    wide, high = q.shape[1] // groups, c.shape[1] // groups
    steps = tokens // QB
    both = groups * (dh + dv)
    half = 2 * (dh + dv)
    f32, b16 = jnp.float32, jnp.bfloat16
    at = 2 * pair
    whole = lambda shape: pl.BlockSpec(shape, lambda g: (0,) * len(shape))
    return pl.pallas_call(
        functools.partial(win_kernel, dh=dh, dv=dv, pair=pair),
        grid=(2,),
        in_specs=[
            pl.BlockSpec(memory_space=pltpu.SMEM),
            pl.BlockSpec((tokens, wide), lambda g: (0, at + g)),
            pl.BlockSpec((tokens, high), lambda g: (0, at + g)),
            pl.BlockSpec((1, 2 * steps, 256), lambda g: (at + g, 0, 0)),
            pl.BlockSpec((tokens, 2 * dh), lambda g: (0, pair)),
            pl.BlockSpec((tokens, dv), lambda g: (0, at + g)),
            *[whole((tokens, both))] * 4,
            pl.BlockSpec((1, 2 * steps, dv, 256), lambda g: (at + g, 0, 0, 0)),
            pl.BlockSpec((1, steps, 2 * dh, 256), lambda g: (at + g, 0, 0, 0)),
            *[pl.BlockSpec(memory_space=pl.ANY)] * len(before),
        ],
        out_specs=[
            pl.BlockSpec((tokens, high), lambda g: (0, at + g)),
            pl.BlockSpec((tokens, wide), lambda g: (0, at + g)),
            pl.BlockSpec((1, 2 * steps, 256), lambda g: (g, 0, 0)),
            whole((WIN, half)),
            whole((tokens, half)),
        ],
        out_shape=[
            jax.ShapeDtypeStruct(c.shape, b16),
            jax.ShapeDtypeStruct(q.shape, b16),
            jax.ShapeDtypeStruct((2, 2 * steps, 256), f32),
            jax.ShapeDtypeStruct((WIN, half), b16),
            jax.ShapeDtypeStruct((tokens, half), f32),
        ],
        scratch_shapes=scratch(WIN + tokens, dh, dv, True),
        input_output_aliases={12: 0, 13: 1} if before else {},
        compiler_params=pltpu.CompilerParams(dimension_semantics=("arbitrary",), vmem_limit_bytes=56 * 2**20),
        cost_estimate=pl.CostEstimate(flops=320 * tokens * 64 * 1920, transcendentals=320 * tokens * 64, bytes_accessed=30_000_000),
        name="attend_win",
    )(start, q, c, gate, k, v, *halos, oc, dqc, *before)


def split_lanes(pair, dh, odd):
    lane = lax.broadcasted_iota(jnp.int32, (pair.shape[0], 256), 1)
    if odd:
        return jnp.where(lane >= 256 - dh, pair[:, 128:], 0.0)
    return jnp.where(lane < dh, pair[:, :256], 0.0)


def to_left(x, dh):
    return pltpu.roll(x, dh, 1)


def to_right(x, dh):
    return pltpu.roll(x, 256 - dh, 1)


def joined(left, right):
    return jnp.concatenate([left[:, :128], left[:, 128:] + right[:, :128], right[:, 128:]], axis=1)


def compress_kernel(k_ref, v_ref, prior_ref, wk_ref, wv_ref, out_ref, ext, y_scr, *, dh, dv, groups):
    tokens, kw = k_ref.shape
    tiles = ext.shape[0]
    for n in range(tiles):
        at = n * 128
        ext[n, :BLK, :] = prior_ref[:, at : at + 128].astype(jnp.float32)
        ref, at = (k_ref, at) if at < kw else (v_ref, at - kw)
        ext[n, BLK:, :] = ref[:, at : at + 128].astype(jnp.float32)

    def every(p):
        return jnp.concatenate([ext[n, pl.ds(p, blocks, stride=STRIDE), :] for n in range(tiles)], axis=1)

    blocks = tokens // STRIDE
    acc_k = jnp.zeros((groups * blocks, dh), jnp.float32)
    acc_v = jnp.zeros((groups * blocks, dv), jnp.float32)
    for p in range(0, BLK, 2):
        one, two = every(p), every(p + 1)
        rows = []
        for g in range(groups):
            at = (g // 2) * 2 * dh
            if g % 2 == 0:
                left = split_lanes(one[:, at : at + 2 * dh], dh, False)
                right = to_right(split_lanes(two[:, at : at + 2 * dh], dh, False), dh)
            else:
                left = to_left(split_lanes(one[:, at : at + 2 * dh], dh, True), dh)
                right = split_lanes(two[:, at : at + 2 * dh], dh, True)
            rows.append(joined(left, right))
        acc_k += nt(jnp.concatenate(rows, axis=0).astype(jnp.bfloat16), wk_ref[:, p * dh : (p + 2) * dh])
        vals = [
            jnp.concatenate([x[:, kw + g * dv : kw + (g + 1) * dv] for x in (one, two)], axis=1) for g in range(groups)
        ]
        acc_v += nn(jnp.concatenate(vals, axis=0).astype(jnp.bfloat16), wv_ref[p * dv : (p + 2) * dv, :])
    y_scr[...] = jnp.zeros_like(y_scr)
    y_scr[:, :dh] = acc_k
    for m in range(groups // 2):
        left = y_scr[2 * m * blocks : (2 * m + 1) * blocks, :]
        right = to_right(y_scr[(2 * m + 1) * blocks : (2 * m + 2) * blocks, :], dh)
        out_ref[:, 2 * m * dh : 2 * (m + 1) * dh] = joined(left, right).astype(jnp.bfloat16)
    for g in range(groups):
        out_ref[:, kw + g * dv : kw + (g + 1) * dv] = acc_v[g * blocks : (g + 1) * blocks].astype(jnp.bfloat16)


def compress(keys, values, prior, wk_t, wv, groups):
    dh, dv = wk_t.shape[0], wv.shape[1]
    blocks = keys.shape[0] // STRIDE
    both = keys.shape[1] + values.shape[1]
    return pl.pallas_call(
        functools.partial(compress_kernel, dh=dh, dv=dv, groups=groups),
        out_shape=jax.ShapeDtypeStruct((blocks, both), jnp.bfloat16),
        scratch_shapes=[
            pltpu.VMEM((both // 128, BLK + keys.shape[0], 128), jnp.float32),
            pltpu.VMEM((groups * blocks, 256), jnp.float32),
        ],
        compiler_params=pltpu.CompilerParams(vmem_limit_bytes=40 * 2**20),
        name="compress",
    )(keys, values, prior, wk_t, wv)


def back_kernel(shard_ref, grads_ref, rows_ref, wk_ref, wv_ref, part_ref, back_ref, wide, spread, *, dh, dv, groups):
    blocks, both = grads_ref.shape
    kw = groups * dh
    chunks = back_ref.shape[0] // STRIDE
    wide[:blocks, :] = grads_ref[...].astype(jnp.float32)
    wide[blocks:, :] = jnp.zeros((wide.shape[0] - blocks, both), jnp.float32)
    shard = shard_ref[0]
    lined = jnp.where(shard < STRIDE, wide[2 : blocks + 2, :], wide[1 : blocks + 1, :]).astype(jnp.bfloat16)
    flipped = rows_ref[...].astype(jnp.float32).T.astype(jnp.bfloat16)
    square = jnp.zeros((2 * dh, 2 * dh), jnp.float32)
    for m in range(groups // 2):
        at = 2 * m * dh
        square += nn(flipped[at : at + 2 * dh], lined[:, at : at + 2 * dh])
    low = square[:dh, :256] + to_left(split_lanes(square[dh:], dh, True), dh)
    part_v = jnp.zeros((dv, dv), jnp.float32)
    for g in range(groups):
        at = kw + g * dv
        part_v += nn(flipped[at : at + dv], lined[:, at : at + dv])
    part_ref[:, :256] = low.astype(jnp.bfloat16)
    part_ref[:dv, 256:] = part_v.astype(jnp.bfloat16)
    part_ref[dv:, 256:] = jnp.zeros((dh - dv, dv), jnp.bfloat16)
    here = wide[pl.ds(pl.multiple_of(shard * chunks, 8), chunks + 8), :]
    near, far = here[1 : chunks + 1], here[2 : chunks + 2]

    def stacked(x):
        rows = []
        for g in range(groups):
            half = split_lanes(x[:, (g // 2) * 2 * dh : (g // 2 + 1) * 2 * dh], dh, g % 2 == 1)
            rows.append(half if g % 2 == 0 else to_left(half, dh))
        return jnp.concatenate(rows, axis=0)[:, :dh].astype(jnp.bfloat16)

    far_k, near_k = stacked(far), stacked(near)
    vals = lambda x: jnp.concatenate([x[:, kw + g * dv : kw + (g + 1) * dv] for g in range(groups)], axis=0).astype(jnp.bfloat16)
    far_v, near_v = vals(far), vals(near)
    span = STRIDE * dh
    for p in range(0, STRIDE, 2):
        at = p * dh
        got = nn(far_k, wk_ref[:, at : at + 2 * dh]) + nn(near_k, wk_ref[:, span + at : span + at + 2 * dh])
        for m in range(groups // 2):
            a = got[2 * m * chunks : (2 * m + 1) * chunks]
            b = got[(2 * m + 1) * chunks : (2 * m + 2) * chunks]
            one = joined(split_lanes(a, dh, False), to_right(split_lanes(b, dh, False), dh))
            two = joined(to_left(split_lanes(a, dh, True), dh), split_lanes(b, dh, True))
            for n in range(3):
                lanes = slice(n * 128, n * 128 + 128)
                spread[3 * m + n, pl.ds(p, chunks, stride=STRIDE), :] = one[:, lanes]
                spread[3 * m + n, pl.ds(p + 1, chunks, stride=STRIDE), :] = two[:, lanes]
    for p in range(STRIDE):
        at = p * dv
        got = nt(far_v, wv_ref[at : at + dv, :]) + nt(near_v, wv_ref[STRIDE * dv + at : STRIDE * dv + at + dv, :])
        for g in range(groups):
            spread[kw // 128 + g, pl.ds(p, chunks, stride=STRIDE), :] = got[g * chunks : (g + 1) * chunks]
    for n in range(spread.shape[0]):
        back_ref[:, n * 128 : n * 128 + 128] = spread[n]


def compress_back(shard, grads, rows, wk_t, wv, tokens, groups):
    dh, dv = wk_t.shape[0], wv.shape[1]
    blocks, both = grads.shape
    vmem = pl.BlockSpec(memory_space=pltpu.VMEM)
    return pl.pallas_call(
        functools.partial(back_kernel, dh=dh, dv=dv, groups=groups),
        in_specs=[pl.BlockSpec(memory_space=pltpu.SMEM), vmem, vmem, vmem, vmem],
        out_shape=[
            jax.ShapeDtypeStruct((dh, 256 + dv), jnp.bfloat16),
            jax.ShapeDtypeStruct((tokens, both), jnp.float32),
        ],
        scratch_shapes=[
            pltpu.VMEM((blocks + 16, both), jnp.float32),
            pltpu.VMEM((both // 128, tokens, 128), jnp.float32),
        ],
        compiler_params=pltpu.CompilerParams(vmem_limit_bytes=40 * 2**20),
        name="compress_back",
    )(shard, grads, rows, wk_t, wv)


def gate_rows(gate, groups):
    tokens, heads = gate.shape
    cut = gate.reshape(tokens // QB, QB, groups, heads // groups // 2, 2)
    return cut.transpose(2, 0, 4, 3, 1).reshape(groups, 2 * (tokens // QB), -1)


def gate_columns(rows, tokens):
    groups = rows.shape[0]
    cut = rows.reshape(groups, tokens // QB, 2, -1, QB)
    return cut.transpose(1, 4, 0, 3, 2).reshape(tokens, -1)


def shifted(array, axis, by, wrap=False):
    devices = lax.axis_size(axis)
    if wrap:
        pairs = [(i, (i + by) % devices) for i in range(devices)]
    else:
        pairs = [(i, i + by) for i in range(devices) if 0 <= i + by < devices]
    return lax.ppermute(array, axis, pairs)


def to_sibling(array):
    return lax.ppermute(array, "seq", [(i, i ^ 1) for i in range(lax.axis_size("seq"))])


def between_chips(array):
    devices = lax.axis_size("seq")
    rings = [list(range(k, devices, 2)) for k in range(2)]
    return lax.all_to_all(array, "seq", 0, 0, axis_index_groups=rings, tiled=True)


def gathered(array, core):
    chips = lax.axis_size("seq") // 2
    mine = between_chips(jnp.broadcast_to(array[None], (chips, *array.shape)))
    other = to_sibling(mine)
    both = jnp.where(core == 0, jnp.stack([mine, other], axis=1), jnp.stack([other, mine], axis=1))
    return both.reshape(-1, array.shape[1])


def whole_step(queries, keys_in, values_in, gate_cmp, gate_win, cotangent, compress_key, compress_value):
    dh, dv = compress_key.shape[1], compress_value.shape[1]
    q, c, keys, values = queries[0], cotangent[0], keys_in[0], values_in[0]
    tokens, kw = keys.shape
    groups = kw // dh
    shard = lax.axis_index("seq").astype(jnp.int32).reshape(1)
    shards = lax.axis_size("seq")
    core = lax.axis_index("seq") % 2
    wk_t = compress_key.T
    last = jnp.concatenate([keys[tokens - BLK :], values[tokens - BLK :]], axis=1)
    prior = shifted(last, "seq", 1)
    own = jnp.concatenate([keys, values], axis=1)
    both = own.shape[1]
    cmp_own = compress(keys, values, prior, wk_t, compress_value, groups)
    cmp_all = gathered(cmp_own, core)
    held, _ = lax.optimization_barrier((own, cmp_own))
    two = shifted(held, "seq", 2)
    four = shifted(held, "seq", 4)
    one = to_sibling(jnp.where(core == 0, own, two))
    three = to_sibling(jnp.where(core == 0, two, four))
    halos = [four, three, two, one]
    first = shard * tokens
    start = jnp.maximum(WIN - first, 0)
    oc, dqc, ggc, gkc = attend_cmp(first, q, c, gate_rows(gate_cmp[0], groups), cmp_all, groups, dh, dv)
    mate = to_sibling(own)
    chip = jnp.where(core == 0, jnp.stack([own, mate]), jnp.stack([mate, own]))
    chip = chip.reshape(2 * tokens // STRIDE, STRIDE // 2, 2, both)
    residue = jnp.where(core == 0, chip[:, :, 0], chip[:, :, 1]).transpose(1, 0, 2)
    residue = jnp.concatenate([residue, residue], axis=0)
    gkc = gkc.reshape(shards // 2, 2, -1, both)
    blocks_dev = gkc.shape[2]
    folded = to_sibling(jnp.where(core == 0, gkc[:, 1], gkc[:, 0]))
    folded = folded.astype(jnp.float32) + jnp.where(core == 0, gkc[:, 0], gkc[:, 1]).astype(jnp.float32)
    sent = jnp.concatenate([folded.astype(jnp.bfloat16), residue], axis=1)
    got = between_chips(sent)
    gckb = jnp.sum(got[:, :blocks_dev].astype(jnp.float32), axis=0).astype(jnp.bfloat16)
    rows = got[:, blocks_dev:].reshape(-1, both)
    grads = gathered(gckb, core)
    win = functools.partial(attend_win, start, q, c, gate_rows(gate_win[0], groups), keys, values, halos, oc, dqc, groups, dh, dv)
    keeps, leads, ggw, out = [], [], [], ()
    for pair in range(groups // 2):
        *out, gg, gh, keep = win(pair, tuple(out))
        ggw.append(gg)
        leads.append(gh)
        keeps.append(keep)
    pieces = [jnp.concatenate([gh[n * tokens : (n + 1) * tokens] for gh in leads], axis=1) for n in range(4)]
    near, nearest = to_sibling(pieces[1]), to_sibling(pieces[3])
    near, nearest = near.astype(jnp.float32), nearest.astype(jnp.float32)
    to_two = (pieces[2].astype(jnp.float32) + jnp.where(core == 0, near, nearest)).astype(jnp.bfloat16)
    to_four = (pieces[0].astype(jnp.float32) + jnp.where(core == 0, 0.0, near)).astype(jnp.bfloat16)
    from_four, from_two = shifted(to_four, "seq", -4), shifted(to_two, "seq", -2)
    keep = jnp.concatenate(keeps, axis=1) + jnp.where(core == 0, nearest, 0.0)
    keep = keep + from_two.astype(jnp.float32) + from_four.astype(jnp.float32)
    half = 2 * (dh + dv)
    keys_back = jnp.concatenate([keep[:, at : at + 2 * dh] for at in (0, half)], axis=1)
    values_back = jnp.concatenate([keep[:, at + 2 * dh : at + half] for at in (0, half)], axis=1)
    attended, grad_query = out
    part, back = compress_back(shard, grads, rows, wk_t, compress_value, tokens, groups)
    parts = [shifted(part, "dp", by, True).astype(jnp.float32) for by in (1, 2, 3)]
    total = (part.astype(jnp.float32) + parts[1]) + (parts[0] + parts[2])
    grad_key = keys_back + back[:, :kw]
    grad_value = values_back + back[:, kw:]
    return (
        attended[None],
        grad_query[None],
        grad_key.astype(jnp.bfloat16)[None],
        grad_value.astype(jnp.bfloat16)[None],
        gate_columns(ggc, tokens)[None],
        gate_columns(jnp.concatenate(ggw, axis=0), tokens)[None],
        total[:, :dh],
        total[:dv, 256:],
    )


def solution(mesh):
    split, copied, rows = P("dp", "seq", None), P(), P("seq", None)
    return jax.shard_map(
        whole_step,
        mesh=mesh,
        in_specs=(split,) * 6 + (copied,) * 2,
        out_specs=(split,) * 6 + (rows,) * 2,
        check_vma=False,
    )
```

```python
import functools
import functools
import math
import jax
import jax.numpy as jnp
from jax import lax
from jax.experimental import pallas as pl
from jax.experimental.pallas import tpu as pltpu
from jax.sharding import PartitionSpec as P


BLK = 32
STRIDE = 16
WIN = 512
NEG = -1e30
QB = 32


def stack_rows(ref, row, width, starts):
    parts = [ref[row : row + QB, at : at + width] for at in starts]
    return jnp.concatenate(parts, axis=0)


def nt(a, b):
    return lax.dot_general(a, b, (((1,), (1,)), ((), ())), preferred_element_type=jnp.float32)


def nn(a, b):
    return lax.dot_general(a, b, (((1,), (0,)), ((), ())), preferred_element_type=jnp.float32)


def lay_keys(pair, ke, ko, kt, rows, odd_group, dh):
    def even():
        lane = lax.broadcasted_iota(jnp.int32, (pair.shape[0], 256), 1)
        src = pair[:, :256].astype(jnp.float32)
        low = jnp.where(lane < dh, src, 0.0)
        ke[rows, :] = low.astype(jnp.bfloat16)
        ko[rows, :] = pltpu.roll(low, 256 - dh, 1).astype(jnp.bfloat16)
        kt[:, rows] = low.T[:dh].astype(jnp.bfloat16)

    def odd():
        lane = lax.broadcasted_iota(jnp.int32, (pair.shape[0], 256), 1)
        src = pair[:, 128:].astype(jnp.float32)
        high = jnp.where(lane >= 256 - dh, src, 0.0)
        low = pltpu.roll(high, dh, 1)
        ko[rows, :] = high.astype(jnp.bfloat16)
        ke[rows, :] = low.astype(jnp.bfloat16)
        kt[:, rows] = low.T[:dh].astype(jnp.bfloat16)

    pl.when(jnp.logical_not(odd_group))(even)
    pl.when(odd_group)(odd)


def join_keys_grad(acc_e, acc_o, scale, dh, odd_group, put):
    def even():
        lane = lax.broadcasted_iota(jnp.int32, acc_e.shape, 1)
        total = (acc_e[...] + pltpu.roll(acc_o[...], dh, 1)) * scale
        put(0, jnp.where(lane < dh, total, 0.0), False)

    def odd():
        lane = lax.broadcasted_iota(jnp.int32, acc_e.shape, 1)
        total = (acc_o[...] + pltpu.roll(acc_e[...], 256 - dh, 1)) * scale
        put(128, jnp.where(lane >= 256 - dh, total, 0.0), True)

    pl.when(jnp.logical_not(odd_group))(even)
    pl.when(odd_group)(odd)


PIECES = 1


class Unit:
    def __init__(self, load, gate, kx, vv, kt, vt, chunks, mask, valid, bufs, acc_k, acc_v, scale, emit):
        self.load, self.gate, self.kx, self.vv, self.kt, self.vt = load, gate, kx, vv, kt, vt
        self.chunks, self.mask, self.valid = chunks, mask, valid
        self.s, self.g, self.p, self.u, self.q, self.c = bufs
        self.acc_k, self.acc_v, self.scale, self.emit = acc_k, acc_v, scale, emit
        self.tops = []
        n = len(chunks)
        cuts = [n * k // PIECES for k in range(PIECES + 1)]
        self.pieces = [chunks[i:j] for i, j in zip(cuts[:-1], cuts[1:])]

    def scores(self):
        def start():
            self.q[...], self.c[...] = self.load()

        def one(piece):
            lo, hi = piece[0][0], piece[-1][1]
            all_s = nt(self.kx[lo:hi, :], self.q[...])
            for at, end in piece:
                s = self.mask(all_s[at - lo : end - lo] * (self.scale * math.log2(math.e)), at, end)
                self.s[at:end, :] = s
                top = jnp.max(s, axis=0, keepdims=True)
                ok = self.valid(at)
                self.tops.append(top if ok is None else jnp.where(ok, top, NEG))

        def two(piece):
            lo, hi = piece[0][0], piece[-1][1]
            self.g[lo:hi, :] = nt(self.vv[lo:hi, :], self.c[...])

        return [start] + [functools.partial(f, piece) for f in (one, two) for piece in self.pieces]

    def weights(self):
        def one(at, end):
            if at == self.chunks[0][0]:
                self.top = functools.reduce(jnp.maximum, self.tops)
                self.norm = jnp.zeros_like(self.top)
                self.mean = jnp.zeros_like(self.top)
            ok = self.valid(at)
            base = self.top if ok is None else jnp.where(ok, self.top, -NEG)
            e = jnp.exp2(self.s[at:end, :] - base)
            self.s[at:end, :] = e
            self.norm = self.norm + jnp.sum(e, axis=0, keepdims=True)
            self.mean = self.mean + jnp.sum(e * self.g[at:end, :], axis=0, keepdims=True)

        return [functools.partial(one, at, end) for at, end in self.chunks]

    def grads(self):
        def one(at, end):
            if at == self.chunks[0][0]:
                self.mean = self.mean / self.norm
                self.weight = self.gate() / self.norm
                for lo, hi in ((0, self.chunks[0][0]), (self.chunks[-1][1], self.s.shape[0])):
                    if hi > lo:
                        self.p[lo:hi, :] = jnp.zeros((hi - lo, 256), jnp.bfloat16)
                        self.u[lo:hi, :] = jnp.zeros((hi - lo, 256), jnp.bfloat16)
            p = self.s[at:end, :] * self.weight
            self.p[at:end, :] = p.astype(jnp.bfloat16)
            self.u[at:end, :] = (p * (self.g[at:end, :] - self.mean)).astype(jnp.bfloat16)

        return [functools.partial(one, at, end) for at, end in self.chunks]

    def results(self):
        def values(piece):
            rows = slice(piece[0][0], piece[-1][1])
            self.acc_v[rows, :] += nn(self.p[rows, :], self.c[...])

        def keys(piece):
            rows = slice(piece[0][0], piece[-1][1])
            self.acc_k[rows, :] += nn(self.u[rows, :], self.q[...])

        def first():
            self.out = nn(self.vt[...], self.p[...])

        def second():
            self.emit(self.out, nn(self.kt[...], self.u[...]) * self.scale, self.mean)

        return [functools.partial(f, piece) for f in (values, keys) for piece in self.pieces] + [first, second]


def merge(one, two):
    steps = [((n + 0.5) / len(x), k, f) for k, x in enumerate((one, two)) for n, f in enumerate(x)]
    return [f for _, _, f in sorted(steps, key=lambda x: x[:2])]


def run_units(units):
    for f in units[0].scores():
        f()
    for n, unit in enumerate(units):
        before = units[n - 1].results() if n else []
        after = units[n + 1].scores() if n + 1 < len(units) else []
        for f in merge(unit.weights() + unit.grads(), before + after):
            f()
    for f in units[-1].results():
        f()


def cmp_kernel(place_ref, q_ref, c_ref, gate_ref, ck_ref, dk_ref, cv_ref, dv_ref, o_ref, dq_ref, gg_ref, gmine_ref, gother_ref,
               ke, ko, vv, kt, vt, s_e, s_o, g_e, g_o, p_e, p_o, u_e, u_o, q_e, q_o, c_e, c_o, acc_e, acc_o, acc_v, acc_w, *, dh, dv):
    group = pl.program_id(0)
    odd_group = group % 2 == 1
    scale = 1.0 / math.sqrt(dh)
    half = ck_ref.shape[0]
    rows = 2 * half
    tokens = q_ref.shape[0]
    for n, (k, v) in enumerate(((ck_ref, cv_ref), (dk_ref, dv_ref))):
        lay_keys(k, ke, ko, kt, slice(n * half, (n + 1) * half), odd_group, dh)
        vv[n * half : (n + 1) * half, :] = v[...]
    vt[...] = vv[...].astype(jnp.float32).T.astype(jnp.bfloat16)
    for acc in (acc_e, acc_o, acc_v, acc_w):
        acc[...] = jnp.zeros_like(acc)
    chunks = [(at, at + 128) for at in range(0, rows, 128)]
    heads = q_ref.shape[1] // dh // 2
    units = []

    def load(row, par):
        return (
            stack_rows(q_ref, row, 256, [2 * dh * h + par * 128 for h in range(heads)]),
            stack_rows(c_ref, row, dv, [(2 * h + par) * dv for h in range(heads)]),
        )

    for block in range(tokens // QB):
        row = block * QB
        lane = lax.broadcasted_iota(jnp.int32, (1, 256), 1) & (QB - 1)
        limit = (place_ref[0] * tokens + row + 1 + lane) // STRIDE

        def mask(s, at, end, limit=limit):
            index = lax.broadcasted_iota(jnp.int32, (end - at, 256), 0)
            owner = place_ref[1] if at < half else 1 - place_ref[1]
            index = 2 * (index - (index & 7)) + (index & 7) + 2 * (at % half) + 8 * owner
            return jnp.where(index <= limit, s, NEG)

        for par, (kx, bufs, acc, accv) in enumerate(
            ((ke, (s_e, g_e, p_e, u_e, q_e, c_e), acc_e, acc_v), (ko, (s_o, g_o, p_o, u_o, q_o, c_o), acc_o, acc_w))
        ):
            at = 2 * block + par

            def emit(out, dq, mean, at=at, block=block, par=par):
                gg_ref[0, at : at + 1, :] = mean
                o_ref[0, at] = out.astype(jnp.bfloat16)
                dq_ref[0, block, par * dh : (par + 1) * dh, :] = dq.astype(jnp.bfloat16)

            units.append(Unit(
                functools.partial(load, row, par),
                functools.partial(lambda at: gate_ref[0, at : at + 1, :], at),
                kx, vv, kt, vt, chunks, mask, lambda at: None, bufs, acc, accv, scale, emit,
            ))
    run_units(units)
    base = pl.multiple_of((group // 2) * 2 * dh, 128)

    def put(at, value, add):
        for ref, part in ((gmine_ref, value[:half]), (gother_ref, value[half:])):
            if add:
                ref[:, pl.ds(base + at, 128)] = (ref[:, pl.ds(base + at, 128)].astype(jnp.float32) + part[:, :128]).astype(jnp.bfloat16)
                ref[:, pl.ds(base + at + 128, 128)] = part[:, 128:].astype(jnp.bfloat16)
            else:
                ref[:, pl.ds(base + at, 256)] = part.astype(jnp.bfloat16)

    join_keys_grad(acc_e, acc_o, scale, dh, odd_group, put)
    at = pl.multiple_of(4 * dh + group * dv, 128)
    total = acc_v[...] + acc_w[...]
    gmine_ref[:, pl.ds(at, dv)] = total[:half].astype(jnp.bfloat16)
    gother_ref[:, pl.ds(at, dv)] = total[half:].astype(jnp.bfloat16)


def win_kernel(place_ref, q_ref, c_ref, gate_ref, k_ref, v_ref, four, four_mate, two, two_mate, mate, oc_ref, dqc_ref, *refs, dh, dv, pair):
    refs = refs[7:] if pair else refs
    halos = ((four, four), (four_mate, two_mate), (two, two), (two_mate, mate))
    win_body(place_ref, q_ref, c_ref, gate_ref, k_ref, v_ref, halos, oc_ref, dqc_ref, *refs, dh=dh, dv=dv, pair=pair)


def win_body(place_ref, q_ref, c_ref, gate_ref, k_ref, v_ref, halo_refs, oc_ref, dqc_ref,
             o_ref, dq_ref, gg_ref, g4_ref, g3_ref, g2_ref, g1_ref, gown_ref,
             ke, ko, vv, kt, vt, s_e, s_o, g_e, g_o, p_e, p_o, u_e, u_o, q_e, q_o, c_e, c_o, acc_e, acc_o, acc_v, acc_w, *, dh, dv, pair):
    odd_group = pl.program_id(0) == 1
    scale = 1.0 / math.sqrt(dh)
    tokens = q_ref.shape[0]
    lead = WIN
    base = pair * 2 * dh
    vbase = pl.multiple_of(4 * dh + (2 * pair + pl.program_id(0)) * dv, 128)
    first_core = place_ref[1] == 0
    for n, (a, b) in enumerate(halo_refs):
        rows = slice(n * tokens, (n + 1) * tokens)
        take = lambda at, width: a[:, pl.ds(at, width)] if a is b else jnp.where(first_core, a[:, pl.ds(at, width)], b[:, pl.ds(at, width)])
        lay_keys(take(base, 2 * dh), ke, ko, kt, rows, odd_group, dh)
        vv[rows, :] = take(vbase, dv)
    lay_keys(k_ref, ke, ko, kt, slice(lead, lead + tokens), odd_group, dh)
    vv[lead:, :] = v_ref[...]
    vt[...] = vv[...].astype(jnp.float32).T.astype(jnp.bfloat16)
    for acc in (acc_e, acc_o, acc_v, acc_w):
        acc[...] = jnp.zeros_like(acc)
    heads = q_ref.shape[1] // dh // 2

    def valid(at):
        return None if at >= lead else at >= lead - place_ref[0] * tokens

    units, halves = [], {}

    def load(row, par):
        return (
            stack_rows(q_ref, row, 256, [2 * dh * h + par * 128 for h in range(heads)]),
            stack_rows(c_ref, row, dv, [(2 * h + par) * dv for h in range(heads)]),
        )

    for block in range(tokens // QB):
        row = block * QB
        edges = sorted({row, row + QB, 128, 256, 384, 512, lead + row, lead + row + QB} - {0})
        edges = [row] + [x for x in edges if row < x <= lead + row + QB]
        chunks = list(zip(edges[:-1], edges[1:]))
        lane = lax.broadcasted_iota(jnp.int32, (QB, 256), 1) & (QB - 1)
        sub = lax.broadcasted_iota(jnp.int32, (QB, 256), 0)

        def mask(s, at, end, row=row, lane=lane, sub=sub):
            if at == row and end == row + QB:
                return jnp.where(sub > lane, s, NEG)
            if at == lead + row:
                return jnp.where(sub <= lane, s, NEG)
            return s

        for par, (kx, bufs, acc, accv) in enumerate(
            ((ke, (s_e, g_e, p_e, u_e, q_e, c_e), acc_e, acc_v), (ko, (s_o, g_o, p_o, u_o, q_o, c_o), acc_o, acc_w))
        ):
            at = 2 * block + par

            def emit(out, dq, mean, at=at, block=block, par=par, row=row):
                gg_ref[0, at : at + 1, :] = mean
                out = (out + oc_ref[0, at].astype(jnp.float32)).T
                for h in range(heads):
                    o_ref[row : row + QB, (2 * h + par) * dv : (2 * h + par + 1) * dv] = out[h * QB : (h + 1) * QB].astype(jnp.bfloat16)
                dq = dq + dqc_ref[0, block, par * dh : (par + 1) * dh, :].astype(jnp.float32)
                if par == 0:
                    halves[block] = dq
                    return
                dq = jnp.concatenate([halves.pop(block), dq], axis=0).T
                for h in range(heads):
                    dq_ref[row : row + QB, 2 * dh * h : 2 * dh * (h + 1)] = dq[h * QB : (h + 1) * QB].astype(jnp.bfloat16)

            units.append(Unit(
                functools.partial(load, row, par),
                functools.partial(lambda at: gate_ref[0, at : at + 1, :], at),
                kx, vv, kt, vt, chunks, mask, valid, bufs, acc, accv, scale, emit,
            ))
    run_units(units)

    def put(at, value, add):
        for n, ref in enumerate((g4_ref, g3_ref, g2_ref, g1_ref, gown_ref)):
            part, kind = value[n * tokens : (n + 1) * tokens], ref.dtype
            if add:
                ref[:, at : at + 128] = (ref[:, at : at + 128].astype(jnp.float32) + part[:, :128]).astype(kind)
                ref[:, at + 128 : at + 256] = part[:, 128:].astype(kind)
            else:
                ref[:, at : at + 256] = part.astype(kind)

    join_keys_grad(acc_e, acc_o, scale, dh, odd_group, put)
    total = acc_v[...] + acc_w[...]
    vat = pl.multiple_of(2 * dh + pl.program_id(0) * dv, 128)
    for n, ref in enumerate((g4_ref, g3_ref, g2_ref, g1_ref, gown_ref)):
        ref[:, pl.ds(vat, dv)] = total[n * tokens : (n + 1) * tokens].astype(ref.dtype)


def scratch(keys, dh, dv):
    f32, b16 = jnp.float32, jnp.bfloat16
    return [
        pltpu.VMEM((keys, 256), b16), pltpu.VMEM((keys, 256), b16),
        pltpu.VMEM((keys, dv), b16),
        pltpu.VMEM((dh, keys), b16), pltpu.VMEM((dv, keys), b16),
        *[pltpu.VMEM((keys, 256), f32)] * 4, *[pltpu.VMEM((keys, 256), b16)] * 4,
        *[pltpu.VMEM((256, 256), b16)] * 2, *[pltpu.VMEM((256, dv), b16)] * 2,
        pltpu.VMEM((keys, 256), f32), pltpu.VMEM((keys, 256), f32),
        pltpu.VMEM((keys, dv), f32), pltpu.VMEM((keys, dv), f32),
    ]


def attend_cmp(place, q, c, gate, mine, other, groups, dh, dv):
    tokens, half = q.shape[0], mine.shape[0]
    blocks = 2 * half
    skip = groups * dh // dv
    wide, high = q.shape[1] // groups, c.shape[1] // groups
    steps = tokens // QB
    f32, b16 = jnp.float32, jnp.bfloat16
    return pl.pallas_call(
        functools.partial(cmp_kernel, dh=dh, dv=dv),
        grid=(groups,),
        in_specs=[
            pl.BlockSpec(memory_space=pltpu.SMEM),
            pl.BlockSpec((tokens, wide), lambda g: (0, g)),
            pl.BlockSpec((tokens, high), lambda g: (0, g)),
            pl.BlockSpec((1, 2 * steps, 256), lambda g: (g, 0, 0)),
            *[pl.BlockSpec((half, 2 * dh), lambda g: (0, g // 2))] * 2,
            *[pl.BlockSpec((half, dv), lambda g: (0, skip + g))] * 2,
        ],
        out_specs=[
            pl.BlockSpec((1, 2 * steps, dv, 256), lambda g: (g, 0, 0, 0)),
            pl.BlockSpec((1, steps, 2 * dh, 256), lambda g: (g, 0, 0, 0)),
            pl.BlockSpec((1, 2 * steps, 256), lambda g: (g, 0, 0)),
            *[pl.BlockSpec((half, groups * (dh + dv)), lambda g: (0, 0))] * 2,
        ],
        out_shape=[
            jax.ShapeDtypeStruct((groups, 2 * steps, dv, 256), b16),
            jax.ShapeDtypeStruct((groups, steps, 2 * dh, 256), b16),
            jax.ShapeDtypeStruct((groups, 2 * steps, 256), f32),
            *[jax.ShapeDtypeStruct((half, groups * (dh + dv)), b16)] * 2,
        ],
        scratch_shapes=scratch(blocks, dh, dv),
        compiler_params=pltpu.CompilerParams(dimension_semantics=("arbitrary",), vmem_limit_bytes=56 * 2**20),
        cost_estimate=pl.CostEstimate(flops=blocks * tokens * 64 * 1920, transcendentals=blocks * tokens * 64, bytes_accessed=30_000_000),
        name="attend_cmp",
    )(place, q, c, gate, mine, other, mine, other)


def attend_win(place, q, c, gate, k, v, halos, oc, dqc, groups, dh, dv, pair, before):
    tokens = q.shape[0]
    wide, high = q.shape[1] // groups, c.shape[1] // groups
    steps = tokens // QB
    both = groups * (dh + dv)
    half = 2 * (dh + dv)
    f32, b16 = jnp.float32, jnp.bfloat16
    at = 2 * pair
    whole = lambda shape: pl.BlockSpec(shape, lambda g: (0,) * len(shape))
    return pl.pallas_call(
        functools.partial(win_kernel, dh=dh, dv=dv, pair=pair),
        grid=(2,),
        in_specs=[
            pl.BlockSpec(memory_space=pltpu.SMEM),
            pl.BlockSpec((tokens, wide), lambda g: (0, at + g)),
            pl.BlockSpec((tokens, high), lambda g: (0, at + g)),
            pl.BlockSpec((1, 2 * steps, 256), lambda g: (at + g, 0, 0)),
            pl.BlockSpec((tokens, 2 * dh), lambda g: (0, pair)),
            pl.BlockSpec((tokens, dv), lambda g: (0, at + g)),
            *[whole((tokens, both))] * 5,
            pl.BlockSpec((1, 2 * steps, dv, 256), lambda g: (at + g, 0, 0, 0)),
            pl.BlockSpec((1, steps, 2 * dh, 256), lambda g: (at + g, 0, 0, 0)),
            *[pl.BlockSpec(memory_space=pl.ANY)] * len(before),
        ],
        out_specs=[
            pl.BlockSpec((tokens, high), lambda g: (0, at + g)),
            pl.BlockSpec((tokens, wide), lambda g: (0, at + g)),
            pl.BlockSpec((1, 2 * steps, 256), lambda g: (g, 0, 0)),
            *[pl.BlockSpec((tokens, half), lambda g: (0, pair))] * 5,
        ],
        out_shape=[
            jax.ShapeDtypeStruct(c.shape, b16),
            jax.ShapeDtypeStruct(q.shape, b16),
            jax.ShapeDtypeStruct((2, 2 * steps, 256), f32),
            *[jax.ShapeDtypeStruct((tokens, both), b16)] * 4,
            jax.ShapeDtypeStruct((tokens, both), f32),
        ],
        scratch_shapes=scratch(WIN + tokens, dh, dv),
        input_output_aliases={13: 0, 14: 1, 15: 3, 16: 4, 17: 5, 18: 6, 19: 7} if before else {},
        compiler_params=pltpu.CompilerParams(dimension_semantics=("arbitrary",), vmem_limit_bytes=56 * 2**20),
        cost_estimate=pl.CostEstimate(flops=320 * tokens * 64 * 1920, transcendentals=320 * tokens * 64, bytes_accessed=30_000_000),
        name="attend_win",
    )(place, q, c, gate, k, v, *halos, oc, dqc, *before)


def split_lanes(pair, dh, odd):
    lane = lax.broadcasted_iota(jnp.int32, (pair.shape[0], 256), 1)
    if odd:
        return jnp.where(lane >= 256 - dh, pair[:, 128:], 0.0)
    return jnp.where(lane < dh, pair[:, :256], 0.0)


def to_left(x, dh):
    return pltpu.roll(x, dh, 1)


def to_right(x, dh):
    return pltpu.roll(x, 256 - dh, 1)


def joined(left, right):
    return jnp.concatenate([left[:, :128], left[:, 128:] + right[:, :128], right[:, 128:]], axis=1)


def compress_kernel(k_ref, v_ref, prior_ref, wk_ref, wv_ref, out_ref, ext, y_scr, *, dh, dv, groups):
    tokens, kw = k_ref.shape
    tiles = ext.shape[0]
    for n in range(tiles):
        at = n * 128
        ext[n, :BLK, :] = prior_ref[:, at : at + 128].astype(jnp.float32)
        ref, at = (k_ref, at) if at < kw else (v_ref, at - kw)
        ext[n, BLK:, :] = ref[:, at : at + 128].astype(jnp.float32)

    def every(p):
        return jnp.concatenate([ext[n, pl.ds(p, blocks, stride=STRIDE), :] for n in range(tiles)], axis=1)

    blocks = tokens // STRIDE
    acc_k = jnp.zeros((groups * blocks, dh), jnp.float32)
    acc_v = jnp.zeros((groups * blocks, dv), jnp.float32)
    for p in range(0, BLK, 2):
        one, two = every(p), every(p + 1)
        rows = []
        for g in range(groups):
            at = (g // 2) * 2 * dh
            if g % 2 == 0:
                left = split_lanes(one[:, at : at + 2 * dh], dh, False)
                right = to_right(split_lanes(two[:, at : at + 2 * dh], dh, False), dh)
            else:
                left = to_left(split_lanes(one[:, at : at + 2 * dh], dh, True), dh)
                right = split_lanes(two[:, at : at + 2 * dh], dh, True)
            rows.append(joined(left, right))
        acc_k += nt(jnp.concatenate(rows, axis=0).astype(jnp.bfloat16), wk_ref[:, p * dh : (p + 2) * dh])
        vals = [
            jnp.concatenate([x[:, kw + g * dv : kw + (g + 1) * dv] for x in (one, two)], axis=1) for g in range(groups)
        ]
        acc_v += nn(jnp.concatenate(vals, axis=0).astype(jnp.bfloat16), wv_ref[p * dv : (p + 2) * dv, :])
    y_scr[...] = jnp.zeros_like(y_scr)
    y_scr[:, :dh] = acc_k
    for m in range(groups // 2):
        left = y_scr[2 * m * blocks : (2 * m + 1) * blocks, :]
        right = to_right(y_scr[(2 * m + 1) * blocks : (2 * m + 2) * blocks, :], dh)
        out_ref[:, 2 * m * dh : 2 * (m + 1) * dh] = joined(left, right).astype(jnp.bfloat16)
    for g in range(groups):
        out_ref[:, kw + g * dv : kw + (g + 1) * dv] = acc_v[g * blocks : (g + 1) * blocks].astype(jnp.bfloat16)


def compress(keys, values, prior, wk_t, wv, groups):
    dh, dv = wk_t.shape[0], wv.shape[1]
    blocks = keys.shape[0] // STRIDE
    both = keys.shape[1] + values.shape[1]
    return pl.pallas_call(
        functools.partial(compress_kernel, dh=dh, dv=dv, groups=groups),
        out_shape=jax.ShapeDtypeStruct((blocks, both), jnp.bfloat16),
        scratch_shapes=[
            pltpu.VMEM((both // 128, BLK + keys.shape[0], 128), jnp.float32),
            pltpu.VMEM((groups * blocks, 256), jnp.float32),
        ],
        compiler_params=pltpu.CompilerParams(vmem_limit_bytes=40 * 2**20),
        name="compress",
    )(keys, values, prior, wk_t, wv)


def back_kernel(place_ref, mine_ref, other_ref, got_ref, wk_ref, wv_ref, part_ref, back_ref, wide, spread, *, dh, dv, groups):
    half, both = mine_ref.shape
    blocks = 2 * half
    kw = groups * dh
    chunks = back_ref.shape[0] // STRIDE
    for ref, owner in ((mine_ref, place_ref[1]), (other_ref, 1 - place_ref[1])):
        value = ref[...].astype(jnp.float32)
        for n in range(0, half, chunks):
            wide[pl.ds(pl.multiple_of(2 * n + chunks * owner, chunks), chunks), :] = value[n : n + chunks]
    wide[blocks:, :] = jnp.zeros((wide.shape[0] - blocks, both), jnp.float32)
    shard = place_ref[0]
    lined = jnp.where(shard < STRIDE, wide[2 : blocks + 2, :], wide[1 : blocks + 1, :]).astype(jnp.bfloat16)
    flipped = got_ref[...].astype(jnp.float32)[:, chunks:].reshape(blocks, both).T.astype(jnp.bfloat16)
    square = jnp.zeros((2 * dh, 2 * dh), jnp.float32)
    for m in range(groups // 2):
        at = 2 * m * dh
        square += nn(flipped[at : at + 2 * dh], lined[:, at : at + 2 * dh])
    low = square[:dh, :256] + to_left(split_lanes(square[dh:], dh, True), dh)
    part_v = jnp.zeros((dv, dv), jnp.float32)
    for g in range(groups):
        at = kw + g * dv
        part_v += nn(flipped[at : at + dv], lined[:, at : at + dv])
    part_ref[:, :256] = low.astype(jnp.bfloat16)
    part_ref[:dv, 256:] = part_v.astype(jnp.bfloat16)
    part_ref[dv:, 256:] = jnp.zeros((dh - dv, dv), jnp.bfloat16)
    here = wide[pl.ds(pl.multiple_of(shard * chunks, 8), chunks + 8), :]
    near, far = here[1 : chunks + 1], here[2 : chunks + 2]

    def stacked(x):
        rows = []
        for g in range(groups):
            half = split_lanes(x[:, (g // 2) * 2 * dh : (g // 2 + 1) * 2 * dh], dh, g % 2 == 1)
            rows.append(half if g % 2 == 0 else to_left(half, dh))
        return jnp.concatenate(rows, axis=0)[:, :dh].astype(jnp.bfloat16)

    far_k, near_k = stacked(far), stacked(near)
    vals = lambda x: jnp.concatenate([x[:, kw + g * dv : kw + (g + 1) * dv] for g in range(groups)], axis=0).astype(jnp.bfloat16)
    far_v, near_v = vals(far), vals(near)
    span = STRIDE * dh
    for p in range(0, STRIDE, 2):
        at = p * dh
        got = nn(far_k, wk_ref[:, at : at + 2 * dh]) + nn(near_k, wk_ref[:, span + at : span + at + 2 * dh])
        for m in range(groups // 2):
            a = got[2 * m * chunks : (2 * m + 1) * chunks]
            b = got[(2 * m + 1) * chunks : (2 * m + 2) * chunks]
            one = joined(split_lanes(a, dh, False), to_right(split_lanes(b, dh, False), dh))
            two = joined(to_left(split_lanes(a, dh, True), dh), split_lanes(b, dh, True))
            for n in range(3):
                lanes = slice(n * 128, n * 128 + 128)
                spread[3 * m + n, pl.ds(p, chunks, stride=STRIDE), :] = one[:, lanes]
                spread[3 * m + n, pl.ds(p + 1, chunks, stride=STRIDE), :] = two[:, lanes]
    for p in range(STRIDE):
        at = p * dv
        got = nt(far_v, wv_ref[at : at + dv, :]) + nt(near_v, wv_ref[STRIDE * dv + at : STRIDE * dv + at + dv, :])
        for g in range(groups):
            spread[kw // 128 + g, pl.ds(p, chunks, stride=STRIDE), :] = got[g * chunks : (g + 1) * chunks]
    for n in range(spread.shape[0]):
        back_ref[:, n * 128 : n * 128 + 128] = spread[n]


def compress_back(place, mine, other, got, wk_t, wv, tokens, groups):
    dh, dv = wk_t.shape[0], wv.shape[1]
    half, both = mine.shape
    vmem = pl.BlockSpec(memory_space=pltpu.VMEM)
    return pl.pallas_call(
        functools.partial(back_kernel, dh=dh, dv=dv, groups=groups),
        in_specs=[pl.BlockSpec(memory_space=pltpu.SMEM), vmem, vmem, vmem, vmem, vmem],
        out_shape=[
            jax.ShapeDtypeStruct((dh, 256 + dv), jnp.bfloat16),
            jax.ShapeDtypeStruct((tokens, both), jnp.float32),
        ],
        scratch_shapes=[
            pltpu.VMEM((2 * half + 16, both), jnp.float32),
            pltpu.VMEM((both // 128, tokens, 128), jnp.float32),
        ],
        compiler_params=pltpu.CompilerParams(vmem_limit_bytes=40 * 2**20),
        name="compress_back",
    )(place, mine, other, got, wk_t, wv)


def gate_rows(gate, groups):
    tokens, heads = gate.shape
    cut = gate.reshape(tokens // QB, QB, groups, heads // groups // 2, 2)
    return cut.transpose(2, 0, 4, 3, 1).reshape(groups, 2 * (tokens // QB), -1)


def gate_columns(rows, tokens):
    groups = rows.shape[0]
    cut = rows.reshape(groups, tokens // QB, 2, -1, QB)
    return cut.transpose(1, 4, 0, 3, 2).reshape(tokens, -1)


def shifted(array, axis, by, wrap=False):
    devices = lax.axis_size(axis)
    if wrap:
        pairs = [(i, (i + by) % devices) for i in range(devices)]
    else:
        pairs = [(i, i + by) for i in range(devices) if 0 <= i + by < devices]
    return lax.ppermute(array, axis, pairs)


def to_sibling(array):
    return lax.ppermute(array, "seq", [(i, i ^ 1) for i in range(lax.axis_size("seq"))])


def between_chips(array):
    devices = lax.axis_size("seq")
    rings = [list(range(k, devices, 2)) for k in range(2)]
    return lax.all_to_all(array, "seq", 0, 0, axis_index_groups=rings, tiled=True)


def gathered(array):
    chips = lax.axis_size("seq") // 2
    mine = between_chips(jnp.broadcast_to(array[None], (chips, *array.shape))).reshape(-1, array.shape[1])
    return mine, to_sibling(mine)


def whole_step(queries, keys_in, values_in, gate_cmp, gate_win, cotangent, compress_key, compress_value):
    dh, dv = compress_key.shape[1], compress_value.shape[1]
    q, c, keys, values = queries[0], cotangent[0], keys_in[0], values_in[0]
    tokens, kw = keys.shape
    groups = kw // dh
    shards = lax.axis_size("seq")
    shard = lax.axis_index("seq").astype(jnp.int32)
    core = shard % 2
    place = jnp.stack([shard, core])
    wk_t = compress_key.T
    last = jnp.concatenate([keys[tokens - BLK :], values[tokens - BLK :]], axis=1)
    prior = shifted(last, "seq", 1)
    cmp_own = compress(keys, values, prior, wk_t, compress_value, groups)
    mine, other = gathered(cmp_own)
    late_keys, late_values, _ = lax.optimization_barrier((keys, values, cmp_own))
    own = jnp.concatenate([late_keys, late_values], axis=1)
    both = own.shape[1]
    two = shifted(own, "seq", 2)
    four = shifted(own, "seq", 4)
    mate = to_sibling(own)
    two_mate = to_sibling(two)
    four_mate = to_sibling(four)
    halos = [four, four_mate, two, two_mate, mate]
    oc, dqc, ggc, gmine, gother = attend_cmp(place, q, c, gate_rows(gate_cmp[0], groups), mine, other, groups, dh, dv)
    chip = jnp.where(core == 0, jnp.stack([own, mate]), jnp.stack([mate, own]))
    chip = chip.reshape(2 * tokens // STRIDE, STRIDE // 2, 2, both)
    residue = jnp.where(core == 0, chip[:, :, 0], chip[:, :, 1]).transpose(1, 0, 2)
    residue = jnp.concatenate([residue, residue], axis=0)
    folded = to_sibling(gother)
    blocks_dev = cmp_own.shape[0]
    folded = (folded.astype(jnp.float32) + gmine.astype(jnp.float32)).astype(jnp.bfloat16)
    sent = jnp.concatenate([folded.reshape(shards // 2, blocks_dev, both), residue], axis=1)
    got = between_chips(sent)
    gckb = jnp.sum(got[:, :blocks_dev].astype(jnp.float32), axis=0).astype(jnp.bfloat16)
    grads = gathered(gckb)
    win = functools.partial(attend_win, place, q, c, gate_rows(gate_win[0], groups), keys, values, halos, oc, dqc, groups, dh, dv)
    ggw, before = [], ()
    for pair in range(groups // 2):
        attended, grad_query, gg, *gk = win(pair, before)
        ggw.append(gg)
        before = (attended, grad_query, *gk)
    to_behind4, to_behind3, to_behind2, to_behind1, keep = gk
    near, nearest = to_sibling(to_behind3), to_sibling(to_behind1)
    near, nearest = near.astype(jnp.float32), nearest.astype(jnp.float32)
    to_four = (to_behind4.astype(jnp.float32) + jnp.where(core == 0, 0.0, near)).astype(jnp.bfloat16)
    to_two = (to_behind2.astype(jnp.float32) + jnp.where(core == 0, near, nearest)).astype(jnp.bfloat16)
    from_four, from_two = shifted(to_four, "seq", -4), shifted(to_two, "seq", -2)
    keep = keep + jnp.where(core == 0, nearest, 0.0)
    keep = keep + from_two.astype(jnp.float32) + from_four.astype(jnp.float32)
    half = 2 * (dh + dv)
    keys_back = jnp.concatenate([keep[:, at : at + 2 * dh] for at in (0, half)], axis=1)
    values_back = jnp.concatenate([keep[:, at + 2 * dh : at + half] for at in (0, half)], axis=1)
    part, back = compress_back(place, *grads, got, wk_t, compress_value, tokens, groups)
    parts = [shifted(part, "dp", by, True).astype(jnp.float32) for by in (1, 2, 3)]
    total = (part.astype(jnp.float32) + parts[1]) + (parts[0] + parts[2])
    grad_key = keys_back + back[:, :kw]
    grad_value = values_back + back[:, kw:]
    return (
        attended[None],
        grad_query[None],
        grad_key.astype(jnp.bfloat16)[None],
        grad_value.astype(jnp.bfloat16)[None],
        gate_columns(ggc, tokens)[None],
        gate_columns(jnp.concatenate(ggw, axis=0), tokens)[None],
        total[:, :dh],
        total[:dv, 256:],
    )


def solution(mesh):
    split, copied, rows = P("dp", "seq", None), P(), P("seq", None)
    return jax.shard_map(
        whole_step,
        mesh=mesh,
        in_specs=(split,) * 6 + (copied,) * 2,
        out_specs=(split,) * 6 + (rows,) * 2,
        check_vma=False,
    )
```

```python
import functools
import functools
import math
import jax
import jax.numpy as jnp
from jax import lax
from jax.experimental import pallas as pl
from jax.experimental.pallas import tpu as pltpu
from jax.sharding import PartitionSpec as P


BLK = 32
STRIDE = 16
WIN = 512
NEG = -1e30
QB = 32


def stack_rows(ref, row, width, starts):
    parts = [ref[row : row + QB, at : at + width] for at in starts]
    return jnp.concatenate(parts, axis=0)


def nt(a, b):
    return lax.dot_general(a, b, (((1,), (1,)), ((), ())), preferred_element_type=jnp.float32)


def nn(a, b):
    return lax.dot_general(a, b, (((1,), (0,)), ((), ())), preferred_element_type=jnp.float32)


def lay_keys(pair, ke, ko, kt, rows, odd_group, dh):
    def even():
        lane = lax.broadcasted_iota(jnp.int32, (pair.shape[0], 256), 1)
        src = pair[:, :256].astype(jnp.float32)
        low = jnp.where(lane < dh, src, 0.0)
        ke[rows, :] = low.astype(jnp.bfloat16)
        ko[rows, :] = pltpu.roll(low, 256 - dh, 1).astype(jnp.bfloat16)
        kt[:, rows] = low.T[:dh].astype(jnp.bfloat16)

    def odd():
        lane = lax.broadcasted_iota(jnp.int32, (pair.shape[0], 256), 1)
        src = pair[:, 128:].astype(jnp.float32)
        high = jnp.where(lane >= 256 - dh, src, 0.0)
        low = pltpu.roll(high, dh, 1)
        ko[rows, :] = high.astype(jnp.bfloat16)
        ke[rows, :] = low.astype(jnp.bfloat16)
        kt[:, rows] = low.T[:dh].astype(jnp.bfloat16)

    pl.when(jnp.logical_not(odd_group))(even)
    pl.when(odd_group)(odd)


def join_keys_grad(acc_e, acc_o, scale, dh, odd_group, put):
    def even():
        lane = lax.broadcasted_iota(jnp.int32, acc_e.shape, 1)
        total = (acc_e[...] + pltpu.roll(acc_o[...], dh, 1)) * scale
        put(0, jnp.where(lane < dh, total, 0.0), False)

    def odd():
        lane = lax.broadcasted_iota(jnp.int32, acc_e.shape, 1)
        total = (acc_o[...] + pltpu.roll(acc_e[...], 256 - dh, 1)) * scale
        put(128, jnp.where(lane >= 256 - dh, total, 0.0), True)

    pl.when(jnp.logical_not(odd_group))(even)
    pl.when(odd_group)(odd)


PIECES = 1


class Unit:
    def __init__(self, load, gate, kx, vv, kt, vt, chunks, mask, valid, bufs, acc_k, acc_v, scale, emit):
        self.load, self.gate, self.kx, self.vv, self.kt, self.vt = load, gate, kx, vv, kt, vt
        self.chunks, self.mask, self.valid = chunks, mask, valid
        self.s, self.g, self.p, self.u, self.q, self.c = bufs
        self.acc_k, self.acc_v, self.scale, self.emit = acc_k, acc_v, scale, emit
        self.tops = []
        n = len(chunks)
        cuts = [n * k // PIECES for k in range(PIECES + 1)]
        self.pieces = [chunks[i:j] for i, j in zip(cuts[:-1], cuts[1:])]

    def scores(self):
        def start():
            self.q[...], self.c[...] = self.load()

        def one(piece):
            lo, hi = piece[0][0], piece[-1][1]
            all_s = nt(self.kx[lo:hi, :], self.q[...])
            for at, end in piece:
                s = self.mask(all_s[at - lo : end - lo] * (self.scale * math.log2(math.e)), at, end)
                self.s[at:end, :] = s
                top = jnp.max(s, axis=0, keepdims=True)
                ok = self.valid(at)
                self.tops.append(top if ok is None else jnp.where(ok, top, NEG))

        def two(piece):
            lo, hi = piece[0][0], piece[-1][1]
            self.g[lo:hi, :] = nt(self.vv[lo:hi, :], self.c[...])

        return [start] + [functools.partial(f, piece) for f in (one, two) for piece in self.pieces]

    def weights(self):
        def one(at, end):
            if at == self.chunks[0][0]:
                self.top = functools.reduce(jnp.maximum, self.tops)
                self.norm = jnp.zeros_like(self.top)
                self.mean = jnp.zeros_like(self.top)
            ok = self.valid(at)
            base = self.top if ok is None else jnp.where(ok, self.top, -NEG)
            e = jnp.exp2(self.s[at:end, :] - base)
            self.s[at:end, :] = e
            self.norm = self.norm + jnp.sum(e, axis=0, keepdims=True)
            self.mean = self.mean + jnp.sum(e * self.g[at:end, :], axis=0, keepdims=True)

        return [functools.partial(one, at, end) for at, end in self.chunks]

    def grads(self):
        def one(at, end):
            if at == self.chunks[0][0]:
                self.mean = self.mean / self.norm
                self.weight = self.gate() / self.norm
                for lo, hi in ((0, self.chunks[0][0]), (self.chunks[-1][1], self.s.shape[0])):
                    if hi > lo:
                        self.p[lo:hi, :] = jnp.zeros((hi - lo, 256), jnp.bfloat16)
                        self.u[lo:hi, :] = jnp.zeros((hi - lo, 256), jnp.bfloat16)
            p = self.s[at:end, :] * self.weight
            self.p[at:end, :] = p.astype(jnp.bfloat16)
            self.u[at:end, :] = (p * (self.g[at:end, :] - self.mean)).astype(jnp.bfloat16)

        return [functools.partial(one, at, end) for at, end in self.chunks]

    def results(self):
        def values(piece):
            rows = slice(piece[0][0], piece[-1][1])
            self.acc_v[rows, :] += nn(self.p[rows, :], self.c[...])

        def keys(piece):
            rows = slice(piece[0][0], piece[-1][1])
            self.acc_k[rows, :] += nn(self.u[rows, :], self.q[...])

        def first():
            self.out = nn(self.vt[...], self.p[...])

        def second():
            self.emit(self.out, nn(self.kt[...], self.u[...]) * self.scale, self.mean)

        return [functools.partial(f, piece) for f in (values, keys) for piece in self.pieces] + [first, second]


def merge(one, two):
    steps = [((n + 0.5) / len(x), k, f) for k, x in enumerate((one, two)) for n, f in enumerate(x)]
    return [f for _, _, f in sorted(steps, key=lambda x: x[:2])]


def run_units(units):
    for f in units[0].scores():
        f()
    for n, unit in enumerate(units):
        before = units[n - 1].results() if n else []
        after = units[n + 1].scores() if n + 1 < len(units) else []
        for f in merge(unit.weights() + unit.grads(), before + after):
            f()
    for f in units[-1].results():
        f()


def cmp_kernel(place_ref, q_ref, c_ref, gate_ref, ck_ref, dk_ref, cv_ref, dv_ref, o_ref, dq_ref, gg_ref, gmine_ref, gother_ref,
               ke, ko, vv, kt, vt, s_e, s_o, g_e, g_o, p_e, p_o, u_e, u_o, q_e, q_o, c_e, c_o, acc_e, acc_o, acc_v, acc_w, *, dh, dv):
    group = pl.program_id(0)
    odd_group = group % 2 == 1
    scale = 1.0 / math.sqrt(dh)
    half = ck_ref.shape[0]
    rows = 2 * half
    tokens = q_ref.shape[0]
    for n, (k, v) in enumerate(((ck_ref, cv_ref), (dk_ref, dv_ref))):
        lay_keys(k, ke, ko, kt, slice(n * half, (n + 1) * half), odd_group, dh)
        vv[n * half : (n + 1) * half, :] = v[...]
    vt[...] = vv[...].astype(jnp.float32).T.astype(jnp.bfloat16)
    for acc in (acc_e, acc_o, acc_v, acc_w):
        acc[...] = jnp.zeros_like(acc)
    chunks = [(at, at + 128) for at in range(0, rows, 128)]
    heads = q_ref.shape[1] // dh // 2
    units = []

    def load(row, par):
        return (
            stack_rows(q_ref, row, 256, [2 * dh * h + par * 128 for h in range(heads)]),
            stack_rows(c_ref, row, dv, [(2 * h + par) * dv for h in range(heads)]),
        )

    for block in range(tokens // QB):
        row = block * QB
        lane = lax.broadcasted_iota(jnp.int32, (1, 256), 1) & (QB - 1)
        limit = (place_ref[0] * tokens + row + 1 + lane) // STRIDE

        def mask(s, at, end, limit=limit):
            index = lax.broadcasted_iota(jnp.int32, (end - at, 256), 0)
            owner = place_ref[1] if at < half else 1 - place_ref[1]
            index = 2 * (index - (index & 7)) + (index & 7) + 2 * (at % half) + 8 * owner
            return jnp.where(index <= limit, s, NEG)

        for par, (kx, bufs, acc, accv) in enumerate(
            ((ke, (s_e, g_e, p_e, u_e, q_e, c_e), acc_e, acc_v), (ko, (s_o, g_o, p_o, u_o, q_o, c_o), acc_o, acc_w))
        ):
            at = 2 * block + par

            def emit(out, dq, mean, at=at, block=block, par=par):
                gg_ref[0, at : at + 1, :] = mean
                o_ref[0, at] = out.astype(jnp.bfloat16)
                dq_ref[0, block, par * dh : (par + 1) * dh, :] = dq.astype(jnp.bfloat16)

            units.append(Unit(
                functools.partial(load, row, par),
                functools.partial(lambda at: gate_ref[0, at : at + 1, :], at),
                kx, vv, kt, vt, chunks, mask, lambda at: None, bufs, acc, accv, scale, emit,
            ))
    run_units(units)
    base = pl.multiple_of((group // 2) * 2 * dh, 128)

    def put(at, value, add):
        for ref, part in ((gmine_ref, value[:half]), (gother_ref, value[half:])):
            if add:
                ref[:, pl.ds(base + at, 128)] = (ref[:, pl.ds(base + at, 128)].astype(jnp.float32) + part[:, :128]).astype(jnp.bfloat16)
                ref[:, pl.ds(base + at + 128, 128)] = part[:, 128:].astype(jnp.bfloat16)
            else:
                ref[:, pl.ds(base + at, 256)] = part.astype(jnp.bfloat16)

    join_keys_grad(acc_e, acc_o, scale, dh, odd_group, put)
    at = pl.multiple_of(4 * dh + group * dv, 128)
    total = acc_v[...] + acc_w[...]
    gmine_ref[:, pl.ds(at, dv)] = total[:half].astype(jnp.bfloat16)
    gother_ref[:, pl.ds(at, dv)] = total[half:].astype(jnp.bfloat16)


def win_kernel(place_ref, q_ref, c_ref, gate_ref, k_ref, v_ref, four, four_mate, two, two_mate, mate, oc_ref, dqc_ref, *refs, dh, dv, pair):
    refs = refs[7:] if pair else refs
    halos = ((four, four), (four_mate, two_mate), (two, two), (two_mate, mate))
    win_body(place_ref, q_ref, c_ref, gate_ref, k_ref, v_ref, halos, oc_ref, dqc_ref, *refs, dh=dh, dv=dv, pair=pair)


def win_body(place_ref, q_ref, c_ref, gate_ref, k_ref, v_ref, halo_refs, oc_ref, dqc_ref,
             o_ref, dq_ref, gg_ref, g4_ref, g3_ref, g2_ref, g1_ref, gown_ref,
             ke, ko, vv, kt, vt, s_e, s_o, g_e, g_o, p_e, p_o, u_e, u_o, q_e, q_o, c_e, c_o, acc_e, acc_o, acc_v, acc_w, *, dh, dv, pair):
    odd_group = pl.program_id(0) == 1
    scale = 1.0 / math.sqrt(dh)
    tokens = q_ref.shape[0]
    lead = WIN
    base = pair * 2 * dh
    vbase = pl.multiple_of(4 * dh + (2 * pair + pl.program_id(0)) * dv, 128)
    first_core = place_ref[1] == 0
    for n, (a, b) in enumerate(halo_refs):
        rows = slice(n * tokens, (n + 1) * tokens)
        take = lambda at, width: a[:, pl.ds(at, width)] if a is b else jnp.where(first_core, a[:, pl.ds(at, width)], b[:, pl.ds(at, width)])
        lay_keys(take(base, 2 * dh), ke, ko, kt, rows, odd_group, dh)
        vv[rows, :] = take(vbase, dv)
    lay_keys(k_ref, ke, ko, kt, slice(lead, lead + tokens), odd_group, dh)
    vv[lead:, :] = v_ref[...]
    vt[...] = vv[...].astype(jnp.float32).T.astype(jnp.bfloat16)
    for acc in (acc_e, acc_o, acc_v, acc_w):
        acc[...] = jnp.zeros_like(acc)
    heads = q_ref.shape[1] // dh // 2

    def valid(at):
        return None if at >= lead else at >= lead - place_ref[0] * tokens

    units, halves = [], {}

    def load(row, par):
        return (
            stack_rows(q_ref, row, 256, [2 * dh * h + par * 128 for h in range(heads)]),
            stack_rows(c_ref, row, dv, [(2 * h + par) * dv for h in range(heads)]),
        )

    for block in range(tokens // QB):
        row = block * QB
        edges = sorted({row, row + QB, 128, 256, 384, 512, lead + row, lead + row + QB} - {0})
        edges = [row] + [x for x in edges if row < x <= lead + row + QB]
        chunks = list(zip(edges[:-1], edges[1:]))
        lane = lax.broadcasted_iota(jnp.int32, (QB, 256), 1) & (QB - 1)
        sub = lax.broadcasted_iota(jnp.int32, (QB, 256), 0)

        def mask(s, at, end, row=row, lane=lane, sub=sub):
            if at == row and end == row + QB:
                return jnp.where(sub > lane, s, NEG)
            if at == lead + row:
                return jnp.where(sub <= lane, s, NEG)
            return s

        for par, (kx, bufs, acc, accv) in enumerate(
            ((ke, (s_e, g_e, p_e, u_e, q_e, c_e), acc_e, acc_v), (ko, (s_o, g_o, p_o, u_o, q_o, c_o), acc_o, acc_w))
        ):
            at = 2 * block + par

            def emit(out, dq, mean, at=at, block=block, par=par, row=row):
                gg_ref[0, at : at + 1, :] = mean
                out = (out + oc_ref[0, at].astype(jnp.float32)).T
                for h in range(heads):
                    o_ref[row : row + QB, (2 * h + par) * dv : (2 * h + par + 1) * dv] = out[h * QB : (h + 1) * QB].astype(jnp.bfloat16)
                dq = dq + dqc_ref[0, block, par * dh : (par + 1) * dh, :].astype(jnp.float32)
                if par == 0:
                    halves[block] = dq
                    return
                dq = jnp.concatenate([halves.pop(block), dq], axis=0).T
                for h in range(heads):
                    dq_ref[row : row + QB, 2 * dh * h : 2 * dh * (h + 1)] = dq[h * QB : (h + 1) * QB].astype(jnp.bfloat16)

            units.append(Unit(
                functools.partial(load, row, par),
                functools.partial(lambda at: gate_ref[0, at : at + 1, :], at),
                kx, vv, kt, vt, chunks, mask, valid, bufs, acc, accv, scale, emit,
            ))
    run_units(units)

    def put(at, value, add):
        for n, ref in enumerate((g4_ref, g3_ref, g2_ref, g1_ref, gown_ref)):
            part, kind = value[n * tokens : (n + 1) * tokens], ref.dtype
            if add:
                ref[:, at : at + 128] = (ref[:, at : at + 128].astype(jnp.float32) + part[:, :128]).astype(kind)
                ref[:, at + 128 : at + 256] = part[:, 128:].astype(kind)
            else:
                ref[:, at : at + 256] = part.astype(kind)

    join_keys_grad(acc_e, acc_o, scale, dh, odd_group, put)
    total = acc_v[...] + acc_w[...]
    vat = pl.multiple_of(2 * dh + pl.program_id(0) * dv, 128)
    for n, ref in enumerate((g4_ref, g3_ref, g2_ref, g1_ref, gown_ref)):
        ref[:, pl.ds(vat, dv)] = total[n * tokens : (n + 1) * tokens].astype(ref.dtype)


def scratch(keys, dh, dv):
    f32, b16 = jnp.float32, jnp.bfloat16
    return [
        pltpu.VMEM((keys, 256), b16), pltpu.VMEM((keys, 256), b16),
        pltpu.VMEM((keys, dv), b16),
        pltpu.VMEM((dh, keys), b16), pltpu.VMEM((dv, keys), b16),
        *[pltpu.VMEM((keys, 256), f32)] * 4, *[pltpu.VMEM((keys, 256), b16)] * 4,
        *[pltpu.VMEM((256, 256), b16)] * 2, *[pltpu.VMEM((256, dv), b16)] * 2,
        pltpu.VMEM((keys, 256), f32), pltpu.VMEM((keys, 256), f32),
        pltpu.VMEM((keys, dv), f32), pltpu.VMEM((keys, dv), f32),
    ]


def attend_cmp(place, q, c, gate, mine, other, groups, dh, dv):
    tokens, half = q.shape[0], mine.shape[0]
    blocks = 2 * half
    skip = groups * dh // dv
    wide, high = q.shape[1] // groups, c.shape[1] // groups
    steps = tokens // QB
    f32, b16 = jnp.float32, jnp.bfloat16
    return pl.pallas_call(
        functools.partial(cmp_kernel, dh=dh, dv=dv),
        grid=(groups,),
        in_specs=[
            pl.BlockSpec(memory_space=pltpu.SMEM),
            pl.BlockSpec((tokens, wide), lambda g: (0, g)),
            pl.BlockSpec((tokens, high), lambda g: (0, g)),
            pl.BlockSpec((1, 2 * steps, 256), lambda g: (g, 0, 0)),
            *[pl.BlockSpec((half, 2 * dh), lambda g: (0, g // 2))] * 2,
            *[pl.BlockSpec((half, dv), lambda g: (0, skip + g))] * 2,
        ],
        out_specs=[
            pl.BlockSpec((1, 2 * steps, dv, 256), lambda g: (g, 0, 0, 0)),
            pl.BlockSpec((1, steps, 2 * dh, 256), lambda g: (g, 0, 0, 0)),
            pl.BlockSpec((1, 2 * steps, 256), lambda g: (g, 0, 0)),
            *[pl.BlockSpec((half, groups * (dh + dv)), lambda g: (0, 0))] * 2,
        ],
        out_shape=[
            jax.ShapeDtypeStruct((groups, 2 * steps, dv, 256), b16),
            jax.ShapeDtypeStruct((groups, steps, 2 * dh, 256), b16),
            jax.ShapeDtypeStruct((groups, 2 * steps, 256), f32),
            *[jax.ShapeDtypeStruct((half, groups * (dh + dv)), b16)] * 2,
        ],
        scratch_shapes=scratch(blocks, dh, dv),
        compiler_params=pltpu.CompilerParams(dimension_semantics=("arbitrary",), vmem_limit_bytes=56 * 2**20),
        cost_estimate=pl.CostEstimate(flops=blocks * tokens * 64 * 1920, transcendentals=blocks * tokens * 64, bytes_accessed=30_000_000),
        name="attend_cmp",
    )(place, q, c, gate, mine, other, mine, other)


def attend_win(place, q, c, gate, k, v, halos, oc, dqc, groups, dh, dv, pair, before):
    tokens = q.shape[0]
    wide, high = q.shape[1] // groups, c.shape[1] // groups
    steps = tokens // QB
    both = groups * (dh + dv)
    half = 2 * (dh + dv)
    f32, b16 = jnp.float32, jnp.bfloat16
    at = 2 * pair
    whole = lambda shape: pl.BlockSpec(shape, lambda g: (0,) * len(shape))
    return pl.pallas_call(
        functools.partial(win_kernel, dh=dh, dv=dv, pair=pair),
        grid=(2,),
        in_specs=[
            pl.BlockSpec(memory_space=pltpu.SMEM),
            pl.BlockSpec((tokens, wide), lambda g: (0, at + g)),
            pl.BlockSpec((tokens, high), lambda g: (0, at + g)),
            pl.BlockSpec((1, 2 * steps, 256), lambda g: (at + g, 0, 0)),
            pl.BlockSpec((tokens, 2 * dh), lambda g: (0, pair)),
            pl.BlockSpec((tokens, dv), lambda g: (0, at + g)),
            *[whole((tokens, both))] * 5,
            pl.BlockSpec((1, 2 * steps, dv, 256), lambda g: (at + g, 0, 0, 0)),
            pl.BlockSpec((1, steps, 2 * dh, 256), lambda g: (at + g, 0, 0, 0)),
            *[pl.BlockSpec(memory_space=pl.ANY)] * len(before),
        ],
        out_specs=[
            pl.BlockSpec((tokens, high), lambda g: (0, at + g)),
            pl.BlockSpec((tokens, wide), lambda g: (0, at + g)),
            pl.BlockSpec((1, 2 * steps, 256), lambda g: (g, 0, 0)),
            *[pl.BlockSpec((tokens, half), lambda g: (0, pair))] * 5,
        ],
        out_shape=[
            jax.ShapeDtypeStruct(c.shape, b16),
            jax.ShapeDtypeStruct(q.shape, b16),
            jax.ShapeDtypeStruct((2, 2 * steps, 256), f32),
            *[jax.ShapeDtypeStruct((tokens, both), b16)] * 4,
            jax.ShapeDtypeStruct((tokens, both), f32),
        ],
        scratch_shapes=scratch(WIN + tokens, dh, dv),
        input_output_aliases={13: 0, 14: 1, 15: 3, 16: 4, 17: 5, 18: 6, 19: 7} if before else {},
        compiler_params=pltpu.CompilerParams(dimension_semantics=("arbitrary",), vmem_limit_bytes=56 * 2**20),
        cost_estimate=pl.CostEstimate(flops=320 * tokens * 64 * 1920, transcendentals=320 * tokens * 64, bytes_accessed=30_000_000),
        name="attend_win",
    )(place, q, c, gate, k, v, *halos, oc, dqc, *before)


def split_lanes(pair, dh, odd):
    lane = lax.broadcasted_iota(jnp.int32, (pair.shape[0], 256), 1)
    if odd:
        return jnp.where(lane >= 256 - dh, pair[:, 128:], 0.0)
    return jnp.where(lane < dh, pair[:, :256], 0.0)


def to_left(x, dh):
    return pltpu.roll(x, dh, 1)


def to_right(x, dh):
    return pltpu.roll(x, 256 - dh, 1)


def joined(left, right):
    return jnp.concatenate([left[:, :128], left[:, 128:] + right[:, :128], right[:, 128:]], axis=1)


def pack_kernel(k_ref, v_ref, own_ref, last_ref):
    tokens, kw = k_ref.shape
    own_ref[:, :kw] = k_ref[...]
    own_ref[:, kw:] = v_ref[...]
    last_ref[:, :kw] = k_ref[tokens - BLK :, :]
    last_ref[:, kw:] = v_ref[tokens - BLK :, :]


def pack(keys, values):
    tokens, both = keys.shape[0], keys.shape[1] + values.shape[1]
    return pl.pallas_call(
        pack_kernel,
        out_shape=[jax.ShapeDtypeStruct((n, both), keys.dtype) for n in (tokens, BLK)],
        compiler_params=pltpu.CompilerParams(vmem_limit_bytes=56 * 2**20),
        name="pack",
    )(keys, values)


def fold_kernel(place_ref, mine_ref, other_ref, rows_ref, mate_ref, out_ref):
    chips = out_ref.shape[0]
    blocks = mine_ref.shape[0] // chips
    total = mine_ref[...].astype(jnp.float32) + other_ref[...].astype(jnp.float32)
    rows, mate = rows_ref[...].astype(jnp.float32), mate_ref[...].astype(jnp.float32)
    core = place_ref[1]
    one, two = jnp.where(core == 0, rows, mate), jnp.where(core == 0, mate, rows)
    for chip in range(chips):
        at = slice(chip * blocks, (chip + 1) * blocks)
        of = slice(chip * blocks % rows.shape[0], chip * blocks % rows.shape[0] + blocks)
        out_ref[chip] = jnp.concatenate([total[at], one[of], two[of]], axis=0).astype(jnp.bfloat16)


def fold(place, mine, other, rows, mate, chips):
    vmem = pl.BlockSpec(memory_space=pltpu.VMEM)
    return pl.pallas_call(
        fold_kernel,
        in_specs=[pl.BlockSpec(memory_space=pltpu.SMEM), vmem, vmem, vmem, vmem],
        out_shape=jax.ShapeDtypeStruct((chips, 3 * mine.shape[0] // chips, mine.shape[1]), mine.dtype),
        compiler_params=pltpu.CompilerParams(vmem_limit_bytes=56 * 2**20),
        name="fold",
    )(place, mine, other, rows, mate)


def pass_kernel(place_ref, four_ref, two_ref, near_ref, nearest_ref, to_four_ref, to_two_ref):
    core = place_ref[1]
    near, nearest = near_ref[...].astype(jnp.float32), nearest_ref[...].astype(jnp.float32)
    to_four_ref[...] = (four_ref[...].astype(jnp.float32) + jnp.where(core == 0, 0.0, near)).astype(jnp.bfloat16)
    to_two_ref[...] = (two_ref[...].astype(jnp.float32) + jnp.where(core == 0, near, nearest)).astype(jnp.bfloat16)


def pass_on(place, *arrays):
    vmem = pl.BlockSpec(memory_space=pltpu.VMEM)
    return pl.pallas_call(
        pass_kernel,
        in_specs=[pl.BlockSpec(memory_space=pltpu.SMEM), *[vmem] * 4],
        out_shape=[jax.ShapeDtypeStruct(arrays[0].shape, jnp.bfloat16)] * 2,
        compiler_params=pltpu.CompilerParams(vmem_limit_bytes=56 * 2**20),
        name="pass_on",
    )(place, *arrays)


def final_kernel(place_ref, keep_ref, nearest_ref, two_ref, four_ref, back_ref, gk_ref, gv_ref, *, kspan, vspan):
    core = place_ref[1]
    pairs = gk_ref.shape[1] // kspan
    for pair in range(pairs):
        for ref, at, to, of, width in (
            (gk_ref, 0, pair * kspan, pair * kspan, kspan),
            (gv_ref, kspan, pair * vspan, pairs * kspan + pair * vspan, vspan),
        ):
            lanes = slice(pair * (kspan + vspan) + at, pair * (kspan + vspan) + at + width)
            total = keep_ref[:, lanes] + jnp.where(core == 0, nearest_ref[:, lanes].astype(jnp.float32), 0.0)
            total = total + two_ref[:, lanes].astype(jnp.float32) + four_ref[:, lanes].astype(jnp.float32)
            ref[:, to : to + width] = (total + back_ref[:, of : of + width]).astype(jnp.bfloat16)


def final(place, keep, nearest, two, four, back, groups, dh, dv):
    vmem = pl.BlockSpec(memory_space=pltpu.VMEM)
    tokens = keep.shape[0]
    return pl.pallas_call(
        functools.partial(final_kernel, kspan=2 * dh, vspan=2 * dv),
        in_specs=[pl.BlockSpec(memory_space=pltpu.SMEM), *[vmem] * 5],
        out_shape=[jax.ShapeDtypeStruct((tokens, groups * d), jnp.bfloat16) for d in (dh, dv)],
        compiler_params=pltpu.CompilerParams(vmem_limit_bytes=16 * 2**20),
        name="final",
    )(place, keep, nearest, two, four, back)


def compress_kernel(place_ref, own_ref, prior_ref, wk_ref, wv_ref, out_ref, rows_ref, mates_ref, ext, y_scr, acc_k, acc_v, *, dh, dv, groups, offsets):
    tokens, _ = own_ref.shape
    kw = groups * dh
    tiles = ext.shape[0]
    blocks = tokens // STRIDE
    step = pl.program_id(0)

    @pl.when(step == 0)
    def _():
        for n in range(tiles):
            lanes = slice(n * 128, n * 128 + 128)
            ext[n, :BLK, :] = prior_ref[:, lanes].astype(jnp.float32)
            ext[n, BLK:, :] = own_ref[:, lanes].astype(jnp.float32)
        acc_k[...] = jnp.zeros_like(acc_k)
        acc_v[...] = jnp.zeros_like(acc_v)
        for ref, odd in ((rows_ref, place_ref[1]), (mates_ref, 1 - place_ref[1])):
            for n in range(tiles):
                rows = [ext[n, pl.ds(BLK + at + odd, blocks, stride=STRIDE), :] for at in range(0, STRIDE, 2)]
                ref[:, n * 128 : n * 128 + 128] = jnp.concatenate(rows, axis=0).astype(jnp.bfloat16)

    def every(p):
        return jnp.concatenate([ext[n, pl.ds(step * offsets + p, blocks, stride=STRIDE), :] for n in range(tiles)], axis=1)

    sum_k, sum_v = acc_k[...], acc_v[...]
    for p in range(0, offsets, 2):
        one, two = every(p), every(p + 1)
        rows = []
        for g in range(groups):
            at = (g // 2) * 2 * dh
            if g % 2 == 0:
                left = split_lanes(one[:, at : at + 2 * dh], dh, False)
                right = to_right(split_lanes(two[:, at : at + 2 * dh], dh, False), dh)
            else:
                left = to_left(split_lanes(one[:, at : at + 2 * dh], dh, True), dh)
                right = split_lanes(two[:, at : at + 2 * dh], dh, True)
            rows.append(joined(left, right))
        sum_k += nt(jnp.concatenate(rows, axis=0).astype(jnp.bfloat16), wk_ref[:, p * dh : (p + 2) * dh])
        vals = [
            jnp.concatenate([x[:, kw + g * dv : kw + (g + 1) * dv] for x in (one, two)], axis=1) for g in range(groups)
        ]
        sum_v += nn(jnp.concatenate(vals, axis=0).astype(jnp.bfloat16), wv_ref[p * dv : (p + 2) * dv, :])
    acc_k[...] = sum_k
    acc_v[...] = sum_v

    @pl.when(step == pl.num_programs(0) - 1)
    def _():
        y_scr[...] = jnp.zeros_like(y_scr)
        y_scr[:, :dh] = acc_k[...]
        outs = []
        for m in range(groups // 2):
            left = y_scr[2 * m * blocks : (2 * m + 1) * blocks, :]
            right = to_right(y_scr[(2 * m + 1) * blocks : (2 * m + 2) * blocks, :], dh)
            outs.append(joined(left, right))
        outs += [acc_v[g * blocks : (g + 1) * blocks, :] for g in range(groups)]
        out = jnp.concatenate(outs, axis=1).astype(jnp.bfloat16)
        for n in range(out_ref.shape[0]):
            out_ref[n] = out


def compress(place, own, prior, wk_t, wv, groups, copies):
    dh, dv = wk_t.shape[0], wv.shape[1]
    blocks, both = own.shape[0] // STRIDE, own.shape[1]
    steps = 2
    offsets = BLK // steps
    whole = lambda shape: pl.BlockSpec(shape, lambda i: (0,) * len(shape))
    in_hbm = lambda x: pltpu.with_memory_space_constraint(x, pltpu.HBM)
    return pl.pallas_call(
        functools.partial(compress_kernel, dh=dh, dv=dv, groups=groups, offsets=offsets),
        grid=(steps,),
        in_specs=[
            pl.BlockSpec(memory_space=pltpu.SMEM),
            whole(own.shape),
            whole(prior.shape),
            pl.BlockSpec((dh, offsets * dh), lambda i: (0, i)),
            pl.BlockSpec((offsets * dv, dv), lambda i: (i, 0)),
        ],
        out_specs=[whole((copies, blocks, both)), *[whole((STRIDE // 2 * blocks, both))] * 2],
        out_shape=[
            jax.ShapeDtypeStruct((copies, blocks, both), jnp.bfloat16),
            *[jax.ShapeDtypeStruct((STRIDE // 2 * blocks, both), jnp.bfloat16)] * 2,
        ],
        scratch_shapes=[
            pltpu.VMEM((both // 128, BLK + own.shape[0], 128), jnp.float32),
            pltpu.VMEM((groups * blocks, 256), jnp.float32),
            pltpu.VMEM((groups * blocks, dh), jnp.float32),
            pltpu.VMEM((groups * blocks, dv), jnp.float32),
        ],
        compiler_params=pltpu.CompilerParams(dimension_semantics=("arbitrary",), vmem_limit_bytes=56 * 2**20),
        name="compress",
    )(place, own, prior, in_hbm(wk_t), in_hbm(wv))


def back_kernel(place_ref, mine_ref, other_ref, got_ref, wk_ref, wv_ref, part_ref, back_ref, wide, spread, *, dh, dv, groups):
    half, both = mine_ref.shape
    blocks = 2 * half
    kw = groups * dh
    chunks = back_ref.shape[0] // STRIDE
    for ref, owner in ((mine_ref, place_ref[1]), (other_ref, 1 - place_ref[1])):
        value = ref[...].astype(jnp.float32)
        for n in range(0, half, chunks):
            wide[pl.ds(pl.multiple_of(2 * n + chunks * owner, chunks), chunks), :] = value[n : n + chunks]
    wide[blocks:, :] = jnp.zeros((wide.shape[0] - blocks, both), jnp.float32)
    shard = place_ref[0]
    lined = jnp.where(shard < STRIDE, wide[2 : blocks + 2, :], wide[1 : blocks + 1, :]).astype(jnp.bfloat16)
    flipped = got_ref[...].astype(jnp.float32)[:, chunks:].reshape(blocks, both).T.astype(jnp.bfloat16)
    square = jnp.zeros((2 * dh, 2 * dh), jnp.float32)
    for m in range(groups // 2):
        at = 2 * m * dh
        square += nn(flipped[at : at + 2 * dh], lined[:, at : at + 2 * dh])
    low = square[:dh, :256] + to_left(split_lanes(square[dh:], dh, True), dh)
    part_v = jnp.zeros((dv, dv), jnp.float32)
    for g in range(groups):
        at = kw + g * dv
        part_v += nn(flipped[at : at + dv], lined[:, at : at + dv])
    part_ref[:, :256] = low.astype(jnp.bfloat16)
    part_ref[:dv, 256:] = part_v.astype(jnp.bfloat16)
    part_ref[dv:, 256:] = jnp.zeros((dh - dv, dv), jnp.bfloat16)
    here = wide[pl.ds(pl.multiple_of(shard * chunks, 8), chunks + 8), :]
    near, far = here[1 : chunks + 1], here[2 : chunks + 2]

    def stacked(x):
        rows = []
        for g in range(groups):
            half = split_lanes(x[:, (g // 2) * 2 * dh : (g // 2 + 1) * 2 * dh], dh, g % 2 == 1)
            rows.append(half if g % 2 == 0 else to_left(half, dh))
        return jnp.concatenate(rows, axis=0)[:, :dh].astype(jnp.bfloat16)

    far_k, near_k = stacked(far), stacked(near)
    vals = lambda x: jnp.concatenate([x[:, kw + g * dv : kw + (g + 1) * dv] for g in range(groups)], axis=0).astype(jnp.bfloat16)
    far_v, near_v = vals(far), vals(near)
    span = STRIDE * dh
    for p in range(0, STRIDE, 2):
        at = p * dh
        got = nn(far_k, wk_ref[:, at : at + 2 * dh]) + nn(near_k, wk_ref[:, span + at : span + at + 2 * dh])
        for m in range(groups // 2):
            a = got[2 * m * chunks : (2 * m + 1) * chunks]
            b = got[(2 * m + 1) * chunks : (2 * m + 2) * chunks]
            one = joined(split_lanes(a, dh, False), to_right(split_lanes(b, dh, False), dh))
            two = joined(to_left(split_lanes(a, dh, True), dh), split_lanes(b, dh, True))
            for n in range(3):
                lanes = slice(n * 128, n * 128 + 128)
                spread[3 * m + n, pl.ds(p, chunks, stride=STRIDE), :] = one[:, lanes]
                spread[3 * m + n, pl.ds(p + 1, chunks, stride=STRIDE), :] = two[:, lanes]
    for p in range(STRIDE):
        at = p * dv
        got = nt(far_v, wv_ref[at : at + dv, :]) + nt(near_v, wv_ref[STRIDE * dv + at : STRIDE * dv + at + dv, :])
        for g in range(groups):
            spread[kw // 128 + g, pl.ds(p, chunks, stride=STRIDE), :] = got[g * chunks : (g + 1) * chunks]
    for n in range(spread.shape[0]):
        back_ref[:, n * 128 : n * 128 + 128] = spread[n]


def compress_back(place, mine, other, got, wk_t, wv, tokens, groups):
    dh, dv = wk_t.shape[0], wv.shape[1]
    half, both = mine.shape
    vmem = pl.BlockSpec(memory_space=pltpu.VMEM)
    return pl.pallas_call(
        functools.partial(back_kernel, dh=dh, dv=dv, groups=groups),
        in_specs=[pl.BlockSpec(memory_space=pltpu.SMEM), vmem, vmem, vmem, vmem, vmem],
        out_shape=[
            jax.ShapeDtypeStruct((dh, 256 + dv), jnp.bfloat16),
            jax.ShapeDtypeStruct((tokens, both), jnp.float32),
        ],
        scratch_shapes=[
            pltpu.VMEM((2 * half + 16, both), jnp.float32),
            pltpu.VMEM((both // 128, tokens, 128), jnp.float32),
        ],
        compiler_params=pltpu.CompilerParams(vmem_limit_bytes=16 * 2**20),
        name="compress_back",
    )(place, mine, other, got, wk_t, wv)


def gate_rows(gate, groups):
    tokens, heads = gate.shape
    cut = gate.reshape(tokens // QB, QB, groups, heads // groups // 2, 2)
    return cut.transpose(2, 0, 4, 3, 1).reshape(groups, 2 * (tokens // QB), -1)


def gate_columns(rows, tokens):
    groups = rows.shape[0]
    cut = rows.reshape(groups, tokens // QB, 2, -1, QB)
    return cut.transpose(1, 4, 0, 3, 2).reshape(tokens, -1)


def shifted(array, axis, by, wrap=False):
    devices = lax.axis_size(axis)
    if wrap:
        pairs = [(i, (i + by) % devices) for i in range(devices)]
    else:
        pairs = [(i, i + by) for i in range(devices) if 0 <= i + by < devices]
    return lax.ppermute(array, axis, pairs)


def to_sibling(array):
    return lax.ppermute(array, "seq", [(i, i ^ 1) for i in range(lax.axis_size("seq"))])


def between_chips(array):
    devices = lax.axis_size("seq")
    rings = [list(range(k, devices, 2)) for k in range(2)]
    return lax.all_to_all(array, "seq", 0, 0, axis_index_groups=rings, tiled=True)


def gathered(copies):
    mine = between_chips(copies).reshape(-1, copies.shape[2])
    return mine, to_sibling(mine)


def whole_step(queries, keys_in, values_in, gate_cmp, gate_win, cotangent, compress_key, compress_value):
    dh, dv = compress_key.shape[1], compress_value.shape[1]
    q, c, keys, values = queries[0], cotangent[0], keys_in[0], values_in[0]
    tokens, kw = keys.shape
    groups = kw // dh
    shards = lax.axis_size("seq")
    shard = lax.axis_index("seq").astype(jnp.int32)
    core = shard % 2
    place = jnp.stack([shard, core])
    wk_t = compress_key.T
    own, last = pack(keys, values)
    prior = shifted(last, "seq", 1)
    cmp_own, rows, mate_rows = compress(place, own, prior, wk_t, compress_value, groups, shards // 2)
    mine, other = gathered(cmp_own)
    two = shifted(own, "seq", 2)
    four = shifted(own, "seq", 4)
    mate = to_sibling(own)
    two_mate = to_sibling(two)
    four_mate = to_sibling(four)
    mate_rows = to_sibling(mate_rows)
    gates = [gate_rows(x, groups) for x in lax.optimization_barrier((gate_cmp[0], gate_win[0], cmp_own))[:2]]
    halos = [four, four_mate, two, two_mate, mate]
    oc, dqc, ggc, gmine, gother = attend_cmp(place, q, c, gates[0], mine, other, groups, dh, dv)
    blocks_dev = cmp_own.shape[1]
    folded = to_sibling(gother)
    sent = fold(place, gmine, folded, rows, mate_rows, shards // 2)
    got = between_chips(sent)
    gckb = jnp.sum(got[:, :blocks_dev].astype(jnp.float32), axis=0).astype(jnp.bfloat16)
    grads = gathered(jnp.broadcast_to(gckb[None], cmp_own.shape))
    win = functools.partial(attend_win, place, q, c, gates[1], keys, values, halos, oc, dqc, groups, dh, dv)
    ggw, before = [], ()
    for pair in range(groups // 2):
        attended, grad_query, gg, *gk = win(pair, before)
        ggw.append(gg)
        before = (attended, grad_query, *gk)
    to_behind4, to_behind3, to_behind2, to_behind1, keep = gk
    near, nearest = to_sibling(to_behind3), to_sibling(to_behind1)
    to_four, to_two = pass_on(place, to_behind4, to_behind2, near, nearest)
    from_four, from_two = shifted(to_four, "seq", -4), shifted(to_two, "seq", -2)
    part, back = compress_back(place, *grads, got, wk_t, compress_value, tokens, groups)
    parts = [shifted(part, "dp", by, True).astype(jnp.float32) for by in (1, 2, 3)]
    total = (part.astype(jnp.float32) + parts[1]) + (parts[0] + parts[2])
    ggc, ggw, part = lax.optimization_barrier((ggc, jnp.concatenate(ggw, axis=0), part))
    gate_grads = [gate_columns(x, tokens) for x in (ggc, ggw)]
    total, gate_grads, from_two, from_four = lax.optimization_barrier((total, gate_grads, from_two, from_four))
    grad_key, grad_value = final(place, keep, nearest, from_two, from_four, back, groups, dh, dv)
    return (
        attended[None],
        grad_query[None],
        grad_key[None],
        grad_value[None],
        gate_grads[0][None],
        gate_grads[1][None],
        total[:, :dh],
        total[:dv, 256:],
    )


def solution(mesh):
    split, copied, rows = P("dp", "seq", None), P(), P("seq", None)
    return jax.shard_map(
        whole_step,
        mesh=mesh,
        in_specs=(split,) * 6 + (copied,) * 2,
        out_specs=(split,) * 6 + (rows,) * 2,
        check_vma=False,
    )
```
